32 devices in a mesh: col: 16 (over z, y, x), row: 2 (over core).
Axes of the slice: x: 2, y: 2, z: 4, core: 2. Of those that a mesh axis runs over, the one named last changes fastest.
Arguments:
- cells: float32 [2048, 32, 128], P('row', 'col'), may hold values from -600 to 600
- inducing: float32 [128, 128], replicated, may hold values from -5 to 5
- col_kv: float32 [128, 256], replicated, may hold values from -0.5 to 0.5
- col_query: float32 [128, 128], replicated, may hold values from -0.5 to 0.5
- col_out: float32 [128, 128], replicated, may hold values from -0.5 to 0.5
- back_query: float32 [128, 128], replicated, may hold values from -0.5 to 0.5
- back_kv: float32 [128, 256], replicated, may hold values from -0.5 to 0.5
- back_out: float32 [128, 128], replicated, may hold values from -0.5 to 0.5
- row_qkv: float32 [128, 384], replicated, may hold values from -0.5 to 0.5
- row_out: float32 [128, 128], replicated, may hold values from -0.5 to 0.5
- mlp_up: float32 [128, 512], replicated, may hold values from -0.5 to 0.5
- mlp_bias: float32 [512], replicated, may hold values from -4 to 4
- mlp_down: float32 [512, 128], replicated, may hold values from -0.25 to 0.25
- scales: float32 [3, 4], replicated, may hold values from 1 to 120
Outputs:
- encoded: float32 [2, 1024, 32, 128], P('row', 'col')
The draws below stay inside these ranges and needn't reach their ends.
All inputs are finite; a program needn't handle non-finite values.
Results may differ from the reference program's by a relative error of at most 0.00035.
Values sent between devices are 32-bit elements; how exact they have to be, the bound alone decides.
A program may use at most 64 MiB of HBM per device.

```python
import math
import jax
import jax.numpy as jnp
from jax import lax

CELL_WIDTH = 128
HEADS = 4
HD = 32
INDUCING_VECTORS = 128
FF = 512
ROW_DEV = 1024
C = 32
TABLE_ROWS = 2048
N_COL = 16
N_ROW = 2


def draw_cells(key, part):
    subkeys = jax.random.split(key, 4)
    cell_scale = jnp.exp(jax.random.uniform(subkeys[1], (TABLE_ROWS, C, 1), jnp.float32, 0.0, math.log(10.0)))
    chan_scale = jnp.exp(jax.random.uniform(subkeys[2], (1, 1, CELL_WIDTH), jnp.float32, 0.0, math.log(10.0)))
    col_mean = jax.random.normal(subkeys[3], (1, C, CELL_WIDTH), jnp.float32)
    sample = jax.random.normal(subkeys[0], (TABLE_ROWS, C, CELL_WIDTH), jnp.float32)
    base = sample + col_mean
    base = jnp.clip(base, -6.0, 6.0)
    return base * chan_scale * cell_scale


def draw_scales(key, part):
    subkeys = jax.random.split(key, 1)
    return jnp.exp(jax.random.uniform(subkeys[0], (3, HEADS), jnp.float32, 0.0, math.log(3.0)))


def bell_draw(key, extent, scale, bound, held_as=jnp.bfloat16):
    array = jax.random.normal(key, extent, jnp.float32) * scale
    return jnp.minimum(jnp.maximum(array, -bound), bound).astype(held_as)


def setup_inputs(seed: int = 0) -> dict:
    keys = jax.random.split(jax.random.key(seed), 15)
    cells = draw_cells(jax.random.fold_in(keys[14], 71), 0)
    inducing = bell_draw(keys[1], (INDUCING_VECTORS, CELL_WIDTH), 1.0, 5.0, jnp.float32)
    col_kv = bell_draw(keys[2], (CELL_WIDTH, 2 * CELL_WIDTH), CELL_WIDTH ** -0.5, 0.5, jnp.float32)
    col_query = bell_draw(keys[3], (CELL_WIDTH, CELL_WIDTH), CELL_WIDTH ** -0.5, 0.5, jnp.float32)
    col_out = bell_draw(keys[4], (CELL_WIDTH, CELL_WIDTH), CELL_WIDTH ** -0.5, 0.5, jnp.float32)
    back_query = bell_draw(keys[5], (CELL_WIDTH, CELL_WIDTH), CELL_WIDTH ** -0.5, 0.5, jnp.float32)
    back_kv = bell_draw(keys[6], (CELL_WIDTH, 2 * CELL_WIDTH), CELL_WIDTH ** -0.5, 0.5, jnp.float32)
    back_out = bell_draw(keys[7], (CELL_WIDTH, CELL_WIDTH), CELL_WIDTH ** -0.5, 0.5, jnp.float32)
    row_qkv = bell_draw(keys[8], (CELL_WIDTH, 3 * CELL_WIDTH), CELL_WIDTH ** -0.5, 0.5, jnp.float32)
    row_out = bell_draw(keys[9], (CELL_WIDTH, CELL_WIDTH), CELL_WIDTH ** -0.5, 0.5, jnp.float32)
    mlp_up = bell_draw(keys[10], (CELL_WIDTH, FF), CELL_WIDTH ** -0.5, 0.5, jnp.float32)
    mlp_bias = bell_draw(keys[11], (FF,), 1.0, 4.0, jnp.float32)
    mlp_down = bell_draw(keys[12], (FF, CELL_WIDTH), FF ** -0.5, 0.25, jnp.float32)
    scales = draw_scales(jax.random.fold_in(keys[14], 71), 0)
    return dict(cells=cells, inducing=inducing, col_kv=col_kv, col_query=col_query, col_out=col_out, back_query=back_query, back_kv=back_kv, back_out=back_out, row_qkv=row_qkv, row_out=row_out, mlp_up=mlp_up, mlp_bias=mlp_bias, mlp_down=mlp_down, scales=scales)


highest_score = lax.Precision.HIGHEST
epsilon = 1e-05

def project(left, weight):
    return jnp.einsum('...e,ef->...f', left, weight, precision=highest_score, preferred_element_type=jnp.float32)

def layer_norm(values):
    centered = values - lax.optimization_barrier(jnp.mean(values, axis=-1, keepdims=True))
    return centered * lax.rsqrt(lax.optimization_barrier(jnp.mean(centered * centered, axis=-1, keepdims=True)) + epsilon)

def row_section(row_block, row_qkv, row_out, mlp_up, mlp_bias, mlp_down, factor):
    block_shape = row_block.shape
    model_width = block_shape[-1]
    head_count = factor.shape[0]
    head_size = model_width // head_count
    flat_rows = row_block.reshape((-1,) + block_shape[-2:])
    split_shape = flat_rows.shape[:-1] + (head_count, head_size)
    qkv_all = project(layer_norm(flat_rows), row_qkv)
    row_query = qkv_all[..., :model_width].reshape(split_shape)
    row_keys = qkv_all[..., model_width:2 * model_width].reshape(split_shape)
    row_values = qkv_all[..., 2 * model_width:].reshape(split_shape)
    forward_scores = jnp.einsum('bchd,bkhd->bhck', row_query, row_keys, precision=highest_score) * factor[None, :, None, None]
    forward_weights = jax.nn.softmax(forward_scores, axis=-1)
    mixed = jnp.einsum('bhck,bkhd->bchd', forward_weights, row_values, precision=highest_score).reshape(flat_rows.shape)
    row_state = flat_rows + project(mixed, row_out)
    hidden = jax.nn.gelu(project(layer_norm(row_state), mlp_up) + mlp_bias)
    return (row_state + project(hidden, mlp_down)).reshape(block_shape)

def reference(cells, inducing, col_kv, col_query, col_out, back_query, back_kv, back_out, row_qkv, row_out, mlp_up, mlp_bias, mlp_down, scales):
    scale_factors = scales / math.sqrt(HD)
    inducing_query = project(inducing, col_query).reshape(INDUCING_VECTORS, HEADS, HD)

    def column_section(column_cells):
        normed = layer_norm(column_cells)
        key_value = project(normed, col_kv)
        input_keys = key_value[:, :CELL_WIDTH].reshape(TABLE_ROWS, HEADS, HD)
        input_values = key_value[:, CELL_WIDTH:].reshape(TABLE_ROWS, HEADS, HD)
        forward_scores = jnp.einsum('zxs,cxs->xzc', inducing_query, input_keys, precision=highest_score) * scale_factors[0][:, None, None]
        forward_weights = jax.nn.softmax(forward_scores, axis=-1)
        pooled_summary = jnp.einsum('cvj,jcf->vcf', forward_weights, input_values, precision=highest_score).reshape(INDUCING_VECTORS, CELL_WIDTH)
        summary = inducing + project(pooled_summary, col_out)
        summary_kv = project(summary, back_kv)
        return_keys = summary_kv[:, :CELL_WIDTH].reshape(INDUCING_VECTORS, HEADS, HD)
        return_values = summary_kv[:, CELL_WIDTH:].reshape(INDUCING_VECTORS, HEADS, HD)
        return_query = project(normed, back_query).reshape(TABLE_ROWS, HEADS, HD)
        return_scores = jnp.einsum('log,pog->lop', return_query, return_keys, precision=highest_score) * scale_factors[1][None, :, None]
        return_weights = jax.nn.softmax(return_scores, axis=-1)
        attended_rows = jnp.einsum('ztx,xtj->ztj', return_weights, return_values, precision=highest_score).reshape(TABLE_ROWS, CELL_WIDTH)
        return normed + project(attended_rows, back_out)
    cell_state = jnp.swapaxes(lax.map(column_section, jnp.swapaxes(cells, 0, 1)), 0, 1)
    block_rows = ROW_DEV // N_COL
    blocks = cell_state.reshape(TABLE_ROWS // block_rows, block_rows, C, CELL_WIDTH)

    def finish(row_block):
        return row_section(row_block, row_qkv, row_out, mlp_up, mlp_bias, mlp_down, scale_factors[2])
    encoded = lax.map(finish, blocks)
    return encoded.reshape(N_ROW, ROW_DEV, C, CELL_WIDTH)
```

```python
import functools
import math

import jax
import jax.numpy as jnp
from jax import lax
from jax.experimental import pallas as pl
from jax.experimental.pallas import tpu as pltpu
from jax.sharding import PartitionSpec as P

epsilon = 1e-05
MESH = pl.DeviceIdType.MESH
bf16 = jnp.bfloat16
f32 = jnp.float32

NN = (((1,), (0,)), ((), ()))
NT = (((1,), (1,)), ((), ()))


def split2(x):
    hi = x.astype(bf16)
    return hi, (x - hi.astype(f32)).astype(bf16)


def split3(x):
    hi = x.astype(bf16)
    rest = x - hi.astype(f32)
    mid = rest.astype(bf16)
    return hi, mid, (rest - mid.astype(f32)).astype(bf16)


def bdot(a, b, dims):
    return lax.dot_general(a, b, dims, preferred_element_type=f32)


def left6(x):
    h, m, l = split3(x)
    return jnp.concatenate([h, m, h, m, h, l], axis=1)


def right6(x, axis):
    h, m, l = split3(x)
    return jnp.concatenate([h, h, m, m, l, h], axis=axis)


def lefts(x):
    h, m, l = split3(x)
    return jnp.concatenate([h, m], axis=1), jnp.concatenate([h, l], axis=1)


def rights(x, k):
    h, m, l = split3(x)
    both = jnp.concatenate([h, m], axis=1 - k)
    return jnp.concatenate([both, both], axis=k), jnp.concatenate([l, h], axis=k)


def fold(x):
    n = x.shape[1] // 2
    return x[:, :n] + x[:, n:]


def narrow6(left, right, dims):
    return fold(bdot(left[0], right[0], dims)) + bdot(left[1], right[1], dims)


def dot6(a, b):
    return narrow6(lefts(a), rights(b, 0), NN)


def dot6_nt(a, b):
    return narrow6(lefts(a), rights(b, 1), NT)


def left4(x):
    return jnp.concatenate(split2(x), axis=1)


def right4(x):
    both = jnp.concatenate(split2(x), axis=1)
    return jnp.concatenate([both, both], axis=0)


def left3(x):
    h, m = split2(x)
    return jnp.concatenate([h, m, h], axis=1)


def right3(x):
    h, m = split2(x)
    return jnp.concatenate([h, h, m], axis=0)


def dot3(a, b):
    return bdot(left3(a), right3(b), NN)


def wide3(a, right_both):
    n = right_both.shape[1] // 2
    h, m = split2(a)
    both = bdot(h, right_both, NN)
    return both[:, :n] + both[:, n:] + bdot(m, right_both[:, :n], NN)


def layer_norm(values):
    centered = values - jnp.mean(values, axis=-1, keepdims=True)
    return centered * lax.rsqrt(jnp.mean(centered * centered, axis=-1, keepdims=True) + epsilon)


def plan(row_count):
    if row_count % 8:
        return row_count, 1, row_count, 0
    if row_count <= 16 or row_count % 16:
        return 8, row_count // 8, 8, 0
    return 8, 2, 16, (row_count - 16) // 16


def kernel(
    sizes,
    scales,
    cells_in,
    inducing,
    col_kv,
    col_query,
    col_out,
    back_query,
    back_kv,
    back_out,
    row_qkv_in,
    row_out_in,
    mlp_up_in,
    mlp_bias,
    mlp_down_in,
    out,
    cells,
    row_qkv,
    row_out,
    mlp_up,
    mlp_down,
    normed,
    fold6,
    base_left,
    base_right,
    back_left,
    back_right,
    mine,
    theirs,
    edge_state,
    edge_arrived,
    mid_state,
    mid_arrived,
    up4,
    qk6,
    value4,
    out4,
    down3,
    finished,
    in_sem,
    stat_send,
    stat_recv,
    cell_send,
    cell_recv,
    out_sem,
):
    n_col, n_row, row_dev, col_dev, width, heads, count = sizes
    head_size = width // heads
    row_count = row_dev // n_col
    columns = n_col * col_dev
    edge, n_edge, mid, n_mid = plan(row_count)
    me = lax.axis_index("col")
    group = lax.axis_index("row")
    root = math.log2(math.e) / math.sqrt(head_size)

    loads = [
        pltpu.make_async_copy(source, target, in_sem.at[k])
        for k, (source, target) in enumerate(
            (
                (cells_in, cells),
                (row_qkv_in, row_qkv),
                (row_out_in, row_out),
                (mlp_up_in, mlp_up),
                (mlp_down_in, mlp_down),
            )
        )
    ]
    loads[0].start()

    barrier = pltpu.get_barrier_semaphore()

    def greet(k, carry):
        pl.semaphore_signal(
            barrier, inc=1, device_id={"col": lax.rem(me + k, n_col)}, device_id_type=MESH
        )
        return carry

    lax.fori_loop(1, n_col, greet, 0)
    for k in range(1, n_row):
        pl.semaphore_signal(
            barrier, inc=1, device_id={"row": lax.rem(group + k, n_row)}, device_id_type=MESH
        )
    for load in loads[1:]:
        load.start()

    lane_head = lax.broadcasted_iota(jnp.int32, (1, width), 1) // head_size
    head_mask = [(lane_head == h).astype(f32) for h in range(heads)]

    def blocks(x, row):
        return jnp.concatenate(
            [x * (head_mask[h] * (scales[row, h] * root)) for h in range(heads)], axis=0
        )

    def plain_blocks(x):
        return jnp.concatenate([x * head_mask[h] for h in range(heads)], axis=0)

    query = dot6(inducing[...], col_query[...])
    score_left = left6(dot6_nt(blocks(query, 0), col_kv[:, :width]))
    value_weight = rights(col_kv[:, width:], 0)
    loads[0].wait()
    for c in range(col_dev):
        column = layer_norm(cells[pl.ds(c, row_dev, stride=col_dev), :])
        normed[c] = column.reshape(n_col, row_count, width)
        scores = bdot(score_left, right6(column, 1), NT)
        peak = jnp.max(scores, axis=1, keepdims=True)
        weights = jnp.exp2(scores - peak)
        total = jnp.sum(weights, axis=1, keepdims=True)
        pooled = wide3(weights, jnp.concatenate(split2(column), axis=1))
        values = narrow6(lefts(pooled), value_weight, NN)

        def gather_heads(x):
            return sum(x[h * count : (h + 1) * count] * head_mask[h] for h in range(heads))

        mine[0, c] = gather_heads(values)
        mine[1, c] = gather_heads(total)
        mine[2, c] = gather_heads(peak)

    pl.semaphore_wait(barrier, n_col - 1 + n_row - 1)

    stat_copies = []
    for k in range(1, n_row):
        copy = pltpu.make_async_remote_copy(
            src_ref=mine,
            dst_ref=theirs.at[k - 1],
            send_sem=stat_send.at[k - 1],
            recv_sem=stat_recv.at[k - 1],
            device_id={"row": lax.rem(group + k, n_row)},
            device_id_type=MESH,
        )
        copy.start()
        stat_copies.append(copy)

    both = dot6(jnp.concatenate([col_out[...], inducing[...]], axis=0), back_kv[...])
    keys = dot6_nt(blocks(both[:, :width], 1), back_query[...])
    moves = dot6(plain_blocks(both[:, width:]), back_out[...])

    def part(x, h, k):
        start = h * (width + count) + k * width
        return x[start : start + (count if k else width)]

    for h in range(heads):
        base_left[h * count : (h + 1) * count] = part(keys, h, 1)
        base_right[h * count : (h + 1) * count] = part(moves, h, 1)
    fold6[...] = right6(
        jnp.concatenate(
            [part(keys, h, 0) for h in range(heads)] + [part(moves, h, 0) for h in range(heads)],
            axis=1,
        ),
        0,
    )

    for copy in stat_copies:
        copy.wait()

    joined = []
    for c in range(col_dev):
        top = mine[2, c]
        for k in range(n_row - 1):
            top = jnp.maximum(top, theirs[k, 2, c])
        factor = jnp.exp2(mine[2, c] - top)
        sums, total = mine[0, c] * factor, mine[1, c] * factor
        for k in range(n_row - 1):
            factor = jnp.exp2(theirs[k, 2, c] - top)
            sums = sums + theirs[k, 0, c] * factor
            total = total + theirs[k, 1, c] * factor
        joined.append(sums / total)
    products = bdot(left6(jnp.concatenate(joined, axis=0)), fold6[...], NN)
    for c in range(col_dev):
        product = products[c * count : (c + 1) * count]
        back_left[c] = right6(
            base_left[...]
            + jnp.concatenate(
                [product[:, h * width : (h + 1) * width] for h in range(heads)], axis=0
            ),
            1,
        )
        back_right[c] = jnp.concatenate(
            split2(
                base_right[...]
                + jnp.concatenate(
                    [product[:, (heads + h) * width : (heads + h + 1) * width] for h in range(heads)],
                    axis=0,
                )
            ),
            axis=1,
        )

    def cell_copy(state, arrived, s, index, k):
        peer = lax.rem(me + k, n_col)
        return pltpu.make_async_remote_copy(
            src_ref=state.at[s, peer],
            dst_ref=arrived.at[s, me],
            send_sem=cell_send.at[index],
            recv_sem=cell_recv.at[index],
            device_id={"col": peer},
            device_id_type=MESH,
        )

    def back_step(state, arrived, s, index, start, sub):
        for c in range(col_dev):
            block = normed[c, :, pl.ds(start, sub), :].reshape(n_col * sub, width)
            scores = bdot(left6(block), back_left[c], NT)
            shares = []
            for h in range(heads):
                part = scores[:, h * count : (h + 1) * count]
                part = jnp.exp2(part - jnp.max(part, axis=1, keepdims=True))
                shares.append(part * (1.0 / jnp.sum(part, axis=1, keepdims=True)))
            moved = block + wide3(jnp.concatenate(shares, axis=1), back_right[c])
            state[s, :, c] = moved.reshape(n_col, sub, width)

        def send(k, inner):
            cell_copy(state, arrived, s, index, k).start()
            return inner

        lax.fori_loop(1, n_col, send, 0)
        arrived[s, me] = state[s, me]

    def first_of(s):
        return pl.multiple_of(edge + s * mid, 8)

    def middle_back(s, carry):
        back_step(mid_state, mid_arrived, s, s + 1, first_of(s), mid)
        return carry

    back_step(edge_state, edge_arrived, 0, 0, 0, edge)
    if n_mid:
        lax.fori_loop(0, n_mid, middle_back, 0)
    for e in range(1, n_edge):
        start = row_count - (n_edge - e) * edge
        back_step(edge_state, edge_arrived, e, n_mid + e, start, edge)

    for load in loads[1:]:
        load.wait()
    qkv = row_qkv[...]
    row_scale = sum(head_mask[h] * (scales[2, h] * root) for h in range(heads))
    qk6[...] = right6(
        jnp.concatenate([qkv[:, :width] * row_scale, qkv[:, width : 2 * width]], axis=1), 0
    )
    value4[...] = right4(qkv[:, 2 * width :])
    out4[...] = right4(row_out[...])
    up_h, up_m = split2(mlp_up[...])
    up4[...] = jnp.concatenate([up_h, up_h, up_m], axis=0)
    down3[...] = jnp.concatenate(split2(0.5 * mlp_down[...]), axis=1)

    rows = max(1, 128 // columns)
    size = rows * columns
    place = lax.broadcasted_iota(jnp.int32, (size, size), 0) // columns
    other = lax.broadcasted_iota(jnp.int32, (size, size), 1) // columns
    same_row = place == other
    cube = math.sqrt(2.0 / math.pi)
    bf_mask = [m.astype(bf16) for m in head_mask]

    def out_copy(index, start, sub):
        place = pl.ds(start * columns, sub * columns)
        return pltpu.make_async_copy(finished.at[place], out.at[place], out_sem.at[index])

    def heads_of(x):
        return jnp.concatenate([x * bf_mask[h] for h in range(heads)], axis=0)

    def row_step(arrived, s, index, start, sub):
        pltpu.make_async_copy(
            arrived.at[s, pl.ds(0, n_col - 1)],
            arrived.at[s, pl.ds(0, n_col - 1)],
            cell_recv.at[index],
        ).wait()
        flat = arrived.at[s].reshape(columns * sub, width)
        x = jnp.concatenate(
            [flat[pl.ds(r, columns, stride=sub), :] for r in range(sub)], axis=0
        )
        h, m, l = split3(layer_norm(x))
        both = jnp.concatenate([h, m], axis=1)
        query_keys = bdot(jnp.concatenate([both, both, h, l], axis=1), qk6[...], NN)
        query_h, query_m, query_l = split3(query_keys[:, :width])
        key_h, key_m, key_l = split3(query_keys[:, width:])
        value_h, value_m = split2(fold(bdot(both, value4[...], NN)))
        mixed = []
        for g in range(sub // rows):
            here = slice(g * size, (g + 1) * size)
            left_h = heads_of(query_h[here])
            left_a = jnp.concatenate([left_h, heads_of(query_m[here])], axis=1)
            left_b = jnp.concatenate([left_h, heads_of(query_l[here])], axis=1)
            right_a = jnp.concatenate([key_h[here], key_m[here]], axis=0)
            right_a = jnp.concatenate([right_a, right_a], axis=1)
            right_b = jnp.concatenate([key_l[here], key_h[here]], axis=1)
            scores = fold(bdot(left_a, right_a, NT)) + bdot(left_b, right_b, NT)
            shares, totals = [], 0.0
            for h in range(heads):
                score = jnp.where(same_row, scores[h * size : (h + 1) * size], -1e30)
                score = jnp.exp2(score - jnp.max(score, axis=1, keepdims=True))
                shares.append(score)
                totals = totals + jnp.sum(score, axis=1, keepdims=True) * head_mask[h]
            pooled = wide3(
                jnp.concatenate(shares, axis=1),
                jnp.concatenate([heads_of(value_h[here]), heads_of(value_m[here])], axis=1),
            )
            mixed.append(pooled / totals)
        mixed = jnp.concatenate(mixed, axis=0)
        row_state = x + fold(bdot(left4(mixed), out4[...], NN))
        v = bdot(left3(layer_norm(row_state)), up4[...], NN) + mlp_bias[...]
        hidden = v * (1.0 + jnp.tanh(v * (cube + (cube * 0.044715) * (v * v))))
        finished[pl.ds(start * columns, sub * columns), :] = row_state + wide3(hidden, down3[...])
        out_copy(index, start, sub).start()

    def middle_row(s, carry):
        row_step(mid_arrived, s, s + 1, first_of(s), mid)
        return carry

    row_step(edge_arrived, 0, 0, 0, edge)
    if n_mid:
        lax.fori_loop(0, n_mid, middle_row, 0)
    for e in range(1, n_edge):
        row_step(edge_arrived, e, n_mid + e, row_count - (n_edge - e) * edge, edge)

    def drain(state, s, index, start, sub):
        pltpu.make_async_copy(
            state.at[s, pl.ds(0, n_col - 1)], state.at[s, pl.ds(0, n_col - 1)], cell_send.at[index]
        ).wait()
        out_copy(index, start, sub).wait()

    def middle_drain(s, carry):
        drain(mid_state, s, s + 1, first_of(s), mid)
        return carry

    drain(edge_state, 0, 0, 0, edge)
    if n_mid:
        lax.fori_loop(0, n_mid, middle_drain, 0)
    for e in range(1, n_edge):
        drain(edge_state, e, n_mid + e, row_count - (n_edge - e) * edge, edge)


def body(
    cells,
    inducing,
    col_kv,
    col_query,
    col_out,
    back_query,
    back_kv,
    back_out,
    row_qkv,
    row_out,
    mlp_up,
    mlp_bias,
    mlp_down,
    scales,
):
    row_dev, col_dev, width = cells.shape
    heads = scales.shape[1]
    count = inducing.shape[0]
    n_col = lax.axis_size("col")
    n_row = lax.axis_size("row")
    row_count = row_dev // n_col
    columns = n_col * col_dev
    edge, n_edge, mid, n_mid = plan(row_count)
    chunks = n_edge + n_mid
    hidden = mlp_up.shape[1]
    vmem = pl.BlockSpec(memory_space=pltpu.VMEM)
    hbm = pl.BlockSpec(memory_space=pl.ANY)
    sizes = (n_col, n_row, row_dev, col_dev, width, heads, count)
    peers = max(1, n_row - 1)
    encoded = pl.pallas_call(
        functools.partial(kernel, sizes),
        out_shape=jax.ShapeDtypeStruct((row_count * columns, width), f32),
        in_specs=[pl.BlockSpec(memory_space=pltpu.SMEM), hbm]
        + [vmem] * 7
        + [hbm] * 3
        + [vmem, hbm],
        out_specs=hbm,
        scratch_shapes=[
            pltpu.VMEM((row_dev * col_dev, width), f32),
            pltpu.VMEM((width, 3 * width), f32),
            pltpu.VMEM((width, width), f32),
            pltpu.VMEM((width, hidden), f32),
            pltpu.VMEM((hidden, width), f32),
            pltpu.VMEM((col_dev, n_col, row_count, width), f32),
            pltpu.VMEM((6 * width, 2 * heads * width), bf16),
            pltpu.VMEM((heads * count, width), f32),
            pltpu.VMEM((heads * count, width), f32),
            pltpu.VMEM((col_dev, heads * count, 6 * width), bf16),
            pltpu.VMEM((col_dev, heads * count, 2 * width), bf16),
            pltpu.VMEM((3, col_dev, count, width), f32),
            pltpu.VMEM((peers, 3, col_dev, count, width), f32),
            pltpu.VMEM((n_edge, n_col, col_dev, edge, width), f32),
            pltpu.VMEM((n_edge, n_col, col_dev, edge, width), f32),
            pltpu.VMEM((max(1, n_mid), n_col, col_dev, mid, width), f32),
            pltpu.VMEM((max(1, n_mid), n_col, col_dev, mid, width), f32),
            pltpu.VMEM((3 * width, hidden), bf16),
            pltpu.VMEM((6 * width, 2 * width), bf16),
            pltpu.VMEM((2 * width, 2 * width), bf16),
            pltpu.VMEM((2 * width, 2 * width), bf16),
            pltpu.VMEM((hidden, 2 * width), bf16),
            pltpu.VMEM((row_count * columns, width), f32),
            pltpu.SemaphoreType.DMA((5,)),
            pltpu.SemaphoreType.DMA((peers,)),
            pltpu.SemaphoreType.DMA((peers,)),
            pltpu.SemaphoreType.DMA((chunks,)),
            pltpu.SemaphoreType.DMA((chunks,)),
            pltpu.SemaphoreType.DMA((chunks,)),
        ],
        compiler_params=pltpu.CompilerParams(
            collective_id=0, has_side_effects=True, vmem_limit_bytes=60 * 1024 * 1024
        ),
    )(
        scales,
        cells.reshape(row_dev * col_dev, width),
        inducing,
        col_kv,
        col_query,
        col_out,
        back_query,
        back_kv,
        back_out,
        row_qkv,
        row_out,
        mlp_up,
        mlp_bias.reshape(1, hidden),
        mlp_down,
    )
    return encoded.reshape(1, row_count, columns, width)


def solution(mesh):
    placed = (P("row", "col", None),) + (P(),) * 13
    return jax.shard_map(
        body, mesh=mesh, in_specs=placed, out_specs=P("row", "col", None, None), check_vma=False
    )
```

```python
import functools
import math

import jax
import jax.numpy as jnp
from jax import lax
from jax.experimental import pallas as pl
from jax.experimental.pallas import tpu as pltpu
from jax.sharding import PartitionSpec as P

epsilon = 1e-05
MESH = pl.DeviceIdType.MESH
bf16 = jnp.bfloat16
f32 = jnp.float32

NN = (((1,), (0,)), ((), ()))
NT = (((1,), (1,)), ((), ()))


def split2(x):
    hi = x.astype(bf16)
    return hi, (x - hi.astype(f32)).astype(bf16)


def split3(x):
    hi = x.astype(bf16)
    rest = x - hi.astype(f32)
    mid = rest.astype(bf16)
    return hi, mid, (rest - mid.astype(f32)).astype(bf16)


def bdot(a, b, dims):
    return lax.dot_general(a, b, dims, preferred_element_type=f32)


def left6(x):
    h, m, l = split3(x)
    return jnp.concatenate([h, m, h, m, h, l], axis=1)


def right6(x, axis):
    h, m, l = split3(x)
    return jnp.concatenate([h, h, m, m, l, h], axis=axis)


def lefts(x):
    h, m, l = split3(x)
    return jnp.concatenate([h, m], axis=1), jnp.concatenate([h, l], axis=1)


def rights(x, k):
    h, m, l = split3(x)
    both = jnp.concatenate([h, m], axis=1 - k)
    return jnp.concatenate([both, both], axis=k), jnp.concatenate([l, h], axis=k)


def fold(x):
    n = x.shape[1] // 2
    return x[:, :n] + x[:, n:]


def narrow6(left, right, dims):
    return fold(bdot(left[0], right[0], dims)) + bdot(left[1], right[1], dims)


def dot6(a, b):
    return narrow6(lefts(a), rights(b, 0), NN)


def dot6_nt(a, b):
    return narrow6(lefts(a), rights(b, 1), NT)


def left4(x):
    return jnp.concatenate(split2(x), axis=1)


def right4(x):
    both = jnp.concatenate(split2(x), axis=1)
    return jnp.concatenate([both, both], axis=0)


def left3(x):
    h, m = split2(x)
    return jnp.concatenate([h, m, h], axis=1)


def right3(x):
    h, m = split2(x)
    return jnp.concatenate([h, h, m], axis=0)


def dot3(a, b):
    return bdot(left3(a), right3(b), NN)


def wide3(a, right_both):
    n = right_both.shape[1] // 2
    h, m = split2(a)
    both = bdot(h, right_both, NN)
    return both[:, :n] + both[:, n:] + bdot(m, right_both[:, :n], NN)


def layer_norm(values):
    centered = values - jnp.mean(values, axis=-1, keepdims=True)
    return centered * lax.rsqrt(jnp.mean(centered * centered, axis=-1, keepdims=True) + epsilon)


def plan(row_count):
    if row_count % 8:
        return row_count, 1, row_count, 0
    if row_count <= 16 or row_count % 16:
        return 8, row_count // 8, 8, 0
    return 8, 2, 16, (row_count - 16) // 16


def kernel(
    sizes,
    scales,
    cells_in,
    inducing,
    col_kv,
    col_query,
    col_out,
    back_query,
    back_kv,
    back_out,
    row_qkv_in,
    row_out_in,
    mlp_up_in,
    mlp_bias,
    mlp_down_in,
    out,
    cells,
    row_qkv,
    row_out,
    mlp_up,
    mlp_down,
    normed,
    fold6,
    base_left,
    base_right,
    back_left,
    back_right,
    mine,
    theirs,
    edge_state,
    edge_arrived,
    mid_state,
    mid_arrived,
    up4,
    qk6,
    value4,
    out4,
    down3,
    in_sem,
    stat_send,
    stat_recv,
    cell_send,
    cell_recv,
):
    n_col, n_row, row_dev, col_dev, width, heads, count = sizes
    head_size = width // heads
    row_count = row_dev // n_col
    columns = n_col * col_dev
    edge, n_edge, mid, n_mid = plan(row_count)
    me = lax.axis_index("col")
    group = lax.axis_index("row")
    root = math.log2(math.e) / math.sqrt(head_size)

    loads = [
        pltpu.make_async_copy(source, target, in_sem.at[k])
        for k, (source, target) in enumerate(
            (
                (cells_in, cells),
                (row_qkv_in, row_qkv),
                (row_out_in, row_out),
                (mlp_up_in, mlp_up),
                (mlp_down_in, mlp_down),
            )
        )
    ]
    loads[0].start()

    barrier = pltpu.get_barrier_semaphore()

    def greet(k, carry):
        pl.semaphore_signal(
            barrier, inc=1, device_id={"col": lax.rem(me + k, n_col)}, device_id_type=MESH
        )
        return carry

    lax.fori_loop(1, n_col, greet, 0)
    for k in range(1, n_row):
        pl.semaphore_signal(
            barrier, inc=1, device_id={"row": lax.rem(group + k, n_row)}, device_id_type=MESH
        )
    for load in loads[1:]:
        load.start()

    lane_head = lax.broadcasted_iota(jnp.int32, (1, width), 1) // head_size
    head_mask = [(lane_head == h).astype(f32) for h in range(heads)]

    def blocks(x, row):
        return jnp.concatenate(
            [x * (head_mask[h] * (scales[row, h] * root)) for h in range(heads)], axis=0
        )

    def plain_blocks(x):
        return jnp.concatenate([x * head_mask[h] for h in range(heads)], axis=0)

    query = dot6(inducing[...], col_query[...])
    score_left = left6(dot6_nt(blocks(query, 0), col_kv[:, :width]))
    value_weight = rights(col_kv[:, width:], 0)
    loads[0].wait()
    for c in range(col_dev):
        column = layer_norm(cells[pl.ds(c, row_dev, stride=col_dev), :])
        normed[c] = column.reshape(n_col, row_count, width)
        scores = bdot(score_left, right6(column, 1), NT)
        peak = jnp.max(scores, axis=1, keepdims=True)
        weights = jnp.exp2(scores - peak)
        total = jnp.sum(weights, axis=1, keepdims=True)
        pooled = wide3(weights, jnp.concatenate(split2(column), axis=1))
        values = narrow6(lefts(pooled), value_weight, NN)

        def gather_heads(x):
            return sum(x[h * count : (h + 1) * count] * head_mask[h] for h in range(heads))

        mine[0, c] = gather_heads(values)
        mine[1, c] = gather_heads(total)
        mine[2, c] = gather_heads(peak)

    pl.semaphore_wait(barrier, n_col - 1 + n_row - 1)

    stat_copies = []
    for k in range(1, n_row):
        copy = pltpu.make_async_remote_copy(
            src_ref=mine,
            dst_ref=theirs.at[k - 1],
            send_sem=stat_send.at[k - 1],
            recv_sem=stat_recv.at[k - 1],
            device_id={"row": lax.rem(group + k, n_row)},
            device_id_type=MESH,
        )
        copy.start()
        stat_copies.append(copy)

    both = dot6(jnp.concatenate([col_out[...], inducing[...]], axis=0), back_kv[...])
    keys = dot6_nt(blocks(both[:, :width], 1), back_query[...])
    moves = dot6(plain_blocks(both[:, width:]), back_out[...])

    def part(x, h, k):
        start = h * (width + count) + k * width
        return x[start : start + (count if k else width)]

    for h in range(heads):
        base_left[h * count : (h + 1) * count] = part(keys, h, 1)
        base_right[h * count : (h + 1) * count] = part(moves, h, 1)
    fold6[...] = right6(
        jnp.concatenate(
            [part(keys, h, 0) for h in range(heads)] + [part(moves, h, 0) for h in range(heads)],
            axis=1,
        ),
        0,
    )

    for copy in stat_copies:
        copy.wait()

    joined = []
    for c in range(col_dev):
        top = mine[2, c]
        for k in range(n_row - 1):
            top = jnp.maximum(top, theirs[k, 2, c])
        factor = jnp.exp2(mine[2, c] - top)
        sums, total = mine[0, c] * factor, mine[1, c] * factor
        for k in range(n_row - 1):
            factor = jnp.exp2(theirs[k, 2, c] - top)
            sums = sums + theirs[k, 0, c] * factor
            total = total + theirs[k, 1, c] * factor
        joined.append(sums / total)
    products = bdot(left6(jnp.concatenate(joined, axis=0)), fold6[...], NN)
    for c in range(col_dev):
        product = products[c * count : (c + 1) * count]
        back_left[c] = right6(
            base_left[...]
            + jnp.concatenate(
                [product[:, h * width : (h + 1) * width] for h in range(heads)], axis=0
            ),
            1,
        )
        back_right[c] = jnp.concatenate(
            split2(
                base_right[...]
                + jnp.concatenate(
                    [product[:, (heads + h) * width : (heads + h + 1) * width] for h in range(heads)],
                    axis=0,
                )
            ),
            axis=1,
        )

    def cell_copy(state, arrived, s, index, k):
        peer = lax.rem(me + k, n_col)
        return pltpu.make_async_remote_copy(
            src_ref=state.at[s, peer],
            dst_ref=arrived.at[s, me],
            send_sem=cell_send.at[index],
            recv_sem=cell_recv.at[index],
            device_id={"col": peer},
            device_id_type=MESH,
        )

    def back_step(state, arrived, s, index, start, sub):
        for c in range(col_dev):
            block = normed[c, :, pl.ds(start, sub), :].reshape(n_col * sub, width)
            scores = bdot(left6(block), back_left[c], NT)
            shares = []
            for h in range(heads):
                part = scores[:, h * count : (h + 1) * count]
                part = jnp.exp2(part - jnp.max(part, axis=1, keepdims=True))
                shares.append(part * (1.0 / jnp.sum(part, axis=1, keepdims=True)))
            moved = block + wide3(jnp.concatenate(shares, axis=1), back_right[c])
            state[s, :, c] = moved.reshape(n_col, sub, width)

        def send(k, inner):
            cell_copy(state, arrived, s, index, k).start()
            return inner

        lax.fori_loop(1, n_col, send, 0)
        arrived[s, me] = state[s, me]

    def first_of(s):
        return pl.multiple_of(edge + s * mid, 8)

    def middle_back(s, carry):
        back_step(mid_state, mid_arrived, s, s + 1, first_of(s), mid)
        return carry

    back_step(edge_state, edge_arrived, 0, 0, 0, edge)
    if n_mid:
        lax.fori_loop(0, n_mid, middle_back, 0)
    for e in range(1, n_edge):
        start = row_count - (n_edge - e) * edge
        back_step(edge_state, edge_arrived, e, n_mid + e, start, edge)

    for load in loads[1:]:
        load.wait()
    qkv = row_qkv[...]
    row_scale = sum(head_mask[h] * (scales[2, h] * root) for h in range(heads))
    qk6[...] = right6(
        jnp.concatenate([qkv[:, :width] * row_scale, qkv[:, width : 2 * width]], axis=1), 0
    )
    value4[...] = right4(qkv[:, 2 * width :])
    out4[...] = right4(row_out[...])
    up_h, up_m = split2(mlp_up[...])
    up4[...] = jnp.concatenate([up_h, up_h, up_m], axis=0)
    down3[...] = jnp.concatenate(split2(0.5 * mlp_down[...]), axis=1)

    rows = max(1, 128 // columns)
    size = rows * columns
    place = lax.broadcasted_iota(jnp.int32, (size, size), 0) // columns
    other = lax.broadcasted_iota(jnp.int32, (size, size), 1) // columns
    same_row = place == other
    cube = math.sqrt(2.0 / math.pi)
    bf_mask = [m.astype(bf16) for m in head_mask]

    def heads_of(x):
        return jnp.concatenate([x * bf_mask[h] for h in range(heads)], axis=0)

    def row_step(arrived, s, index, start, sub):
        pltpu.make_async_copy(
            arrived.at[s, pl.ds(0, n_col - 1)],
            arrived.at[s, pl.ds(0, n_col - 1)],
            cell_recv.at[index],
        ).wait()
        flat = arrived.at[s].reshape(columns * sub, width)
        x = jnp.concatenate(
            [flat[pl.ds(r, columns, stride=sub), :] for r in range(sub)], axis=0
        )
        h, m, l = split3(layer_norm(x))
        both = jnp.concatenate([h, m], axis=1)
        query_keys = bdot(jnp.concatenate([both, both, h, l], axis=1), qk6[...], NN)
        query_h, query_m, query_l = split3(query_keys[:, :width])
        key_h, key_m, key_l = split3(query_keys[:, width:])
        value_h, value_m = split2(fold(bdot(both, value4[...], NN)))
        mixed = []
        for g in range(sub // rows):
            here = slice(g * size, (g + 1) * size)
            left_h = heads_of(query_h[here])
            left_a = jnp.concatenate([left_h, heads_of(query_m[here])], axis=1)
            left_b = jnp.concatenate([left_h, heads_of(query_l[here])], axis=1)
            right_a = jnp.concatenate([key_h[here], key_m[here]], axis=0)
            right_a = jnp.concatenate([right_a, right_a], axis=1)
            right_b = jnp.concatenate([key_l[here], key_h[here]], axis=1)
            scores = fold(bdot(left_a, right_a, NT)) + bdot(left_b, right_b, NT)
            shares, totals = [], 0.0
            for h in range(heads):
                score = jnp.where(same_row, scores[h * size : (h + 1) * size], -1e30)
                score = jnp.exp2(score - jnp.max(score, axis=1, keepdims=True))
                shares.append(score)
                totals = totals + jnp.sum(score, axis=1, keepdims=True) * head_mask[h]
            pooled = wide3(
                jnp.concatenate(shares, axis=1),
                jnp.concatenate([heads_of(value_h[here]), heads_of(value_m[here])], axis=1),
            )
            mixed.append(pooled / totals)
        mixed = jnp.concatenate(mixed, axis=0)
        row_state = x + fold(bdot(left4(mixed), out4[...], NN))
        v = bdot(left3(layer_norm(row_state)), up4[...], NN) + mlp_bias[...]
        hidden = v * (1.0 + jnp.tanh(v * (cube + (cube * 0.044715) * (v * v))))
        out[pl.ds(start * columns, sub * columns), :] = row_state + wide3(hidden, down3[...])

    def middle_row(s, carry):
        row_step(mid_arrived, s, s + 1, first_of(s), mid)
        return carry

    row_step(edge_arrived, 0, 0, 0, edge)
    if n_mid:
        lax.fori_loop(0, n_mid, middle_row, 0)
    for e in range(1, n_edge):
        row_step(edge_arrived, e, n_mid + e, row_count - (n_edge - e) * edge, edge)

    def drain(state, s, index, start, sub):
        pltpu.make_async_copy(
            state.at[s, pl.ds(0, n_col - 1)], state.at[s, pl.ds(0, n_col - 1)], cell_send.at[index]
        ).wait()

    def middle_drain(s, carry):
        drain(mid_state, s, s + 1, first_of(s), mid)
        return carry

    drain(edge_state, 0, 0, 0, edge)
    if n_mid:
        lax.fori_loop(0, n_mid, middle_drain, 0)
    for e in range(1, n_edge):
        drain(edge_state, e, n_mid + e, row_count - (n_edge - e) * edge, edge)


def body(
    cells,
    inducing,
    col_kv,
    col_query,
    col_out,
    back_query,
    back_kv,
    back_out,
    row_qkv,
    row_out,
    mlp_up,
    mlp_bias,
    mlp_down,
    scales,
):
    row_dev, col_dev, width = cells.shape
    heads = scales.shape[1]
    count = inducing.shape[0]
    n_col = lax.axis_size("col")
    n_row = lax.axis_size("row")
    row_count = row_dev // n_col
    columns = n_col * col_dev
    edge, n_edge, mid, n_mid = plan(row_count)
    chunks = n_edge + n_mid
    hidden = mlp_up.shape[1]
    vmem = pl.BlockSpec(memory_space=pltpu.VMEM)
    hbm = pl.BlockSpec(memory_space=pl.ANY)
    sizes = (n_col, n_row, row_dev, col_dev, width, heads, count)
    peers = max(1, n_row - 1)
    encoded = pl.pallas_call(
        functools.partial(kernel, sizes),
        out_shape=pltpu.VMEM((row_count * columns, width), f32),
        in_specs=[pl.BlockSpec(memory_space=pltpu.SMEM), hbm]
        + [vmem] * 7
        + [hbm] * 3
        + [vmem, hbm],
        out_specs=vmem,
        scratch_shapes=[
            pltpu.VMEM((row_dev * col_dev, width), f32),
            pltpu.VMEM((width, 3 * width), f32),
            pltpu.VMEM((width, width), f32),
            pltpu.VMEM((width, hidden), f32),
            pltpu.VMEM((hidden, width), f32),
            pltpu.VMEM((col_dev, n_col, row_count, width), f32),
            pltpu.VMEM((6 * width, 2 * heads * width), bf16),
            pltpu.VMEM((heads * count, width), f32),
            pltpu.VMEM((heads * count, width), f32),
            pltpu.VMEM((col_dev, heads * count, 6 * width), bf16),
            pltpu.VMEM((col_dev, heads * count, 2 * width), bf16),
            pltpu.VMEM((3, col_dev, count, width), f32),
            pltpu.VMEM((peers, 3, col_dev, count, width), f32),
            pltpu.VMEM((n_edge, n_col, col_dev, edge, width), f32),
            pltpu.VMEM((n_edge, n_col, col_dev, edge, width), f32),
            pltpu.VMEM((max(1, n_mid), n_col, col_dev, mid, width), f32),
            pltpu.VMEM((max(1, n_mid), n_col, col_dev, mid, width), f32),
            pltpu.VMEM((3 * width, hidden), bf16),
            pltpu.VMEM((6 * width, 2 * width), bf16),
            pltpu.VMEM((2 * width, 2 * width), bf16),
            pltpu.VMEM((2 * width, 2 * width), bf16),
            pltpu.VMEM((hidden, 2 * width), bf16),
            pltpu.SemaphoreType.DMA((5,)),
            pltpu.SemaphoreType.DMA((peers,)),
            pltpu.SemaphoreType.DMA((peers,)),
            pltpu.SemaphoreType.DMA((chunks,)),
            pltpu.SemaphoreType.DMA((chunks,)),
        ],
        compiler_params=pltpu.CompilerParams(
            collective_id=0, has_side_effects=True, vmem_limit_bytes=60 * 1024 * 1024
        ),
    )(
        scales,
        cells.reshape(row_dev * col_dev, width),
        inducing,
        col_kv,
        col_query,
        col_out,
        back_query,
        back_kv,
        back_out,
        row_qkv,
        row_out,
        mlp_up,
        mlp_bias.reshape(1, hidden),
        mlp_down,
    )
    return encoded.reshape(1, row_count, columns, width)


def solution(mesh):
    placed = (P("row", "col", None),) + (P(),) * 13
    return jax.shard_map(
        body, mesh=mesh, in_specs=placed, out_specs=P("row", "col", None, None), check_vma=False
    )
```

```python
import functools
import math

import jax
import jax.numpy as jnp
from jax import lax
from jax.experimental import pallas as pl
from jax.experimental.pallas import tpu as pltpu
from jax.sharding import PartitionSpec as P

epsilon = 1e-05
MESH = pl.DeviceIdType.MESH
bf16 = jnp.bfloat16
f32 = jnp.float32

NN = (((1,), (0,)), ((), ()))
NT = (((1,), (1,)), ((), ()))


def split2(x):
    hi = x.astype(bf16)
    return hi, (x - hi.astype(f32)).astype(bf16)


def split3(x):
    hi = x.astype(bf16)
    rest = x - hi.astype(f32)
    mid = rest.astype(bf16)
    return hi, mid, (rest - mid.astype(f32)).astype(bf16)


def bdot(a, b, dims):
    return lax.dot_general(a, b, dims, preferred_element_type=f32)


def left6(x):
    h, m, l = split3(x)
    return jnp.concatenate([h, m, h, m, h, l], axis=1)


def right6(x, axis):
    h, m, l = split3(x)
    return jnp.concatenate([h, h, m, m, l, h], axis=axis)


def lefts(x):
    h, m, l = split3(x)
    return jnp.concatenate([h, m], axis=1), jnp.concatenate([h, l], axis=1)


def rights(x, k):
    h, m, l = split3(x)
    both = jnp.concatenate([h, m], axis=1 - k)
    return jnp.concatenate([both, both], axis=k), jnp.concatenate([l, h], axis=k)


def fold(x):
    n = x.shape[1] // 2
    return x[:, :n] + x[:, n:]


def narrow6(left, right, dims):
    return fold(bdot(left[0], right[0], dims)) + bdot(left[1], right[1], dims)


def dot6(a, b):
    return narrow6(lefts(a), rights(b, 0), NN)


def dot6_nt(a, b):
    return narrow6(lefts(a), rights(b, 1), NT)


def left4(x):
    return jnp.concatenate(split2(x), axis=1)


def right4(x):
    both = jnp.concatenate(split2(x), axis=1)
    return jnp.concatenate([both, both], axis=0)


def left3(x):
    h, m = split2(x)
    return jnp.concatenate([h, m, h], axis=1)


def right3(x):
    h, m = split2(x)
    return jnp.concatenate([h, h, m], axis=0)


def dot3(a, b):
    return bdot(left3(a), right3(b), NN)


def wide3(a, right_both):
    n = right_both.shape[1] // 2
    h, m = split2(a)
    both = bdot(h, right_both, NN)
    return both[:, :n] + both[:, n:] + bdot(m, right_both[:, :n], NN)


def pipelined(units, ahead, begin, end):
    started, finished = [], []
    for k, unit in enumerate(units):
        started.append(begin(unit))
        if k >= ahead:
            finished.append(end(units[k - ahead], started[k - ahead]))
    for k in range(max(0, len(units) - ahead), len(units)):
        finished.append(end(units[k], started[k]))
    return finished


def layer_norm(values):
    centered = values - jnp.mean(values, axis=-1, keepdims=True)
    return centered * lax.rsqrt(jnp.mean(centered * centered, axis=-1, keepdims=True) + epsilon)


def plan(row_count):
    if row_count % 8:
        return row_count, 1, row_count, 0
    if row_count <= 16 or row_count % 16:
        return 8, row_count // 8, 8, 0
    return 8, 2, 16, (row_count - 16) // 16


def kernel(
    sizes,
    scales,
    cells_in,
    inducing,
    col_kv,
    col_query,
    col_out,
    back_query,
    back_kv,
    back_out,
    row_qkv_in,
    row_out_in,
    mlp_up_in,
    mlp_bias,
    mlp_down_in,
    out,
    cells,
    row_qkv,
    row_out,
    mlp_up,
    mlp_down,
    normed,
    fold6,
    base_left,
    base_right,
    back_left,
    back_right,
    mine,
    theirs,
    edge_state,
    edge_arrived,
    mid_state,
    mid_arrived,
    up4,
    qk6,
    value4,
    out4,
    down3,
    in_sem,
    stat_send,
    stat_recv,
    cell_send,
    cell_recv,
):
    n_col, n_row, row_dev, col_dev, width, heads, count = sizes
    head_size = width // heads
    row_count = row_dev // n_col
    columns = n_col * col_dev
    edge, n_edge, mid, n_mid = plan(row_count)
    me = lax.axis_index("col")
    group = lax.axis_index("row")
    root = math.log2(math.e) / math.sqrt(head_size)

    loads = [
        pltpu.make_async_copy(source, target, in_sem.at[k])
        for k, (source, target) in enumerate(
            (
                (cells_in, cells),
                (row_qkv_in, row_qkv),
                (row_out_in, row_out),
                (mlp_up_in, mlp_up),
                (mlp_down_in, mlp_down),
            )
        )
    ]
    loads[0].start()

    barrier = pltpu.get_barrier_semaphore()

    def greet(k, carry):
        pl.semaphore_signal(
            barrier, inc=1, device_id={"col": lax.rem(me + k, n_col)}, device_id_type=MESH
        )
        return carry

    lax.fori_loop(1, n_col, greet, 0)
    for k in range(1, n_row):
        pl.semaphore_signal(
            barrier, inc=1, device_id={"row": lax.rem(group + k, n_row)}, device_id_type=MESH
        )
    for load in loads[1:]:
        load.start()

    lane_head = lax.broadcasted_iota(jnp.int32, (1, width), 1) // head_size
    head_mask = [(lane_head == h).astype(f32) for h in range(heads)]

    def blocks(x, row):
        return jnp.concatenate(
            [x * (head_mask[h] * (scales[row, h] * root)) for h in range(heads)], axis=0
        )

    def plain_blocks(x):
        return jnp.concatenate([x * head_mask[h] for h in range(heads)], axis=0)

    query = dot6(inducing[...], col_query[...])
    score_left = left6(dot6_nt(blocks(query, 0), col_kv[:, :width]))
    value_weight = rights(col_kv[:, width:], 0)
    loads[0].wait()
    for c in range(col_dev):
        column = layer_norm(cells[pl.ds(c, row_dev, stride=col_dev), :])
        normed[c] = column.reshape(n_col, row_count, width)
        scores = bdot(score_left, right6(column, 1), NT)
        peak = jnp.max(scores, axis=1, keepdims=True)
        weights = jnp.exp2(scores - peak)
        total = jnp.sum(weights, axis=1, keepdims=True)
        pooled = wide3(weights, jnp.concatenate(split2(column), axis=1))
        values = narrow6(lefts(pooled), value_weight, NN)

        def gather_heads(x):
            return sum(x[h * count : (h + 1) * count] * head_mask[h] for h in range(heads))

        mine[0, c] = gather_heads(values)
        mine[1, c] = gather_heads(total)
        mine[2, c] = gather_heads(peak)

    pl.semaphore_wait(barrier, n_col - 1 + n_row - 1)

    stat_copies = []
    for k in range(1, n_row):
        copy = pltpu.make_async_remote_copy(
            src_ref=mine,
            dst_ref=theirs.at[k - 1],
            send_sem=stat_send.at[k - 1],
            recv_sem=stat_recv.at[k - 1],
            device_id={"row": lax.rem(group + k, n_row)},
            device_id_type=MESH,
        )
        copy.start()
        stat_copies.append(copy)

    both = dot6(jnp.concatenate([col_out[...], inducing[...]], axis=0), back_kv[...])
    keys = dot6_nt(blocks(both[:, :width], 1), back_query[...])
    moves = dot6(plain_blocks(both[:, width:]), back_out[...])

    def part(x, h, k):
        start = h * (width + count) + k * width
        return x[start : start + (count if k else width)]

    for h in range(heads):
        base_left[h * count : (h + 1) * count] = part(keys, h, 1)
        base_right[h * count : (h + 1) * count] = part(moves, h, 1)
    fold6[...] = right6(
        jnp.concatenate(
            [part(keys, h, 0) for h in range(heads)] + [part(moves, h, 0) for h in range(heads)],
            axis=1,
        ),
        0,
    )

    for copy in stat_copies:
        copy.wait()

    joined = []
    for c in range(col_dev):
        top = mine[2, c]
        for k in range(n_row - 1):
            top = jnp.maximum(top, theirs[k, 2, c])
        factor = jnp.exp2(mine[2, c] - top)
        sums, total = mine[0, c] * factor, mine[1, c] * factor
        for k in range(n_row - 1):
            factor = jnp.exp2(theirs[k, 2, c] - top)
            sums = sums + theirs[k, 0, c] * factor
            total = total + theirs[k, 1, c] * factor
        joined.append(sums / total)
    products = bdot(left6(jnp.concatenate(joined, axis=0)), fold6[...], NN)
    for c in range(col_dev):
        product = products[c * count : (c + 1) * count]
        back_left[c] = right6(
            base_left[...]
            + jnp.concatenate(
                [product[:, h * width : (h + 1) * width] for h in range(heads)], axis=0
            ),
            1,
        )
        back_right[c] = jnp.concatenate(
            split2(
                base_right[...]
                + jnp.concatenate(
                    [product[:, (heads + h) * width : (heads + h + 1) * width] for h in range(heads)],
                    axis=0,
                )
            ),
            axis=1,
        )

    def cell_copy(state, arrived, s, index, k):
        peer = lax.rem(me + k, n_col)
        return pltpu.make_async_remote_copy(
            src_ref=state.at[s, peer],
            dst_ref=arrived.at[s, me],
            send_sem=cell_send.at[index],
            recv_sem=cell_recv.at[index],
            device_id={"col": peer},
            device_id_type=MESH,
        )

    def back_step(state, arrived, s, index, start, sub):
        def begin_back(c):
            block = normed[c, :, pl.ds(start, sub), :].reshape(n_col * sub, width)
            return block, bdot(left6(block), back_left[c], NT)

        def end_back(c, begun):
            block, scores = begun
            shares = []
            for h in range(heads):
                part = scores[:, h * count : (h + 1) * count]
                part = jnp.exp2(part - jnp.max(part, axis=1, keepdims=True))
                shares.append(part * (1.0 / jnp.sum(part, axis=1, keepdims=True)))
            moved = block + wide3(jnp.concatenate(shares, axis=1), back_right[c])
            state[s, :, c] = moved.reshape(n_col, sub, width)

        pipelined(list(range(col_dev)), 1, begin_back, end_back)

        def send(k, inner):
            cell_copy(state, arrived, s, index, k).start()
            return inner

        lax.fori_loop(1, n_col, send, 0)
        arrived[s, me] = state[s, me]

    def first_of(s):
        return pl.multiple_of(edge + s * mid, 8)

    def middle_back(s, carry):
        back_step(mid_state, mid_arrived, s, s + 1, first_of(s), mid)
        return carry

    back_step(edge_state, edge_arrived, 0, 0, 0, edge)
    if n_mid:
        lax.fori_loop(0, n_mid, middle_back, 0)
    for e in range(1, n_edge):
        start = row_count - (n_edge - e) * edge
        back_step(edge_state, edge_arrived, e, n_mid + e, start, edge)

    for load in loads[1:]:
        load.wait()
    qkv = row_qkv[...]
    row_scale = sum(head_mask[h] * (scales[2, h] * root) for h in range(heads))
    qk6[...] = right6(
        jnp.concatenate([qkv[:, :width] * row_scale, qkv[:, width : 2 * width]], axis=1), 0
    )
    value4[...] = right4(qkv[:, 2 * width :])
    out4[...] = right4(row_out[...])
    up_h, up_m = split2(mlp_up[...])
    up4[...] = jnp.concatenate([up_h, up_h, up_m], axis=0)
    down3[...] = jnp.concatenate(split2(0.5 * mlp_down[...]), axis=1)

    rows = max(1, 128 // columns)
    size = rows * columns
    place = lax.broadcasted_iota(jnp.int32, (size, size), 0) // columns
    other = lax.broadcasted_iota(jnp.int32, (size, size), 1) // columns
    same_row = place == other
    cube = math.sqrt(2.0 / math.pi)
    bf_mask = [m.astype(bf16) for m in head_mask]

    def heads_of(x):
        return jnp.concatenate([x * bf_mask[h] for h in range(heads)], axis=0)

    def row_step(arrived, s, index, start, sub):
        pltpu.make_async_copy(
            arrived.at[s, pl.ds(0, n_col - 1)],
            arrived.at[s, pl.ds(0, n_col - 1)],
            cell_recv.at[index],
        ).wait()
        flat = arrived.at[s].reshape(columns * sub, width)
        x = jnp.concatenate(
            [flat[pl.ds(r, columns, stride=sub), :] for r in range(sub)], axis=0
        )
        h, m, l = split3(layer_norm(x))
        both = jnp.concatenate([h, m], axis=1)
        query_keys = bdot(jnp.concatenate([both, both, h, l], axis=1), qk6[...], NN)
        query_h, query_m, query_l = split3(query_keys[:, :width])
        key_h, key_m, key_l = split3(query_keys[:, width:])
        value_h, value_m = split2(fold(bdot(both, value4[...], NN)))

        def begin_row(g):
            here = slice(g * size, (g + 1) * size)
            left_h = heads_of(query_h[here])
            left_a = jnp.concatenate([left_h, heads_of(query_m[here])], axis=1)
            left_b = jnp.concatenate([left_h, heads_of(query_l[here])], axis=1)
            right_a = jnp.concatenate([key_h[here], key_m[here]], axis=0)
            right_a = jnp.concatenate([right_a, right_a], axis=1)
            right_b = jnp.concatenate([key_l[here], key_h[here]], axis=1)
            return fold(bdot(left_a, right_a, NT)) + bdot(left_b, right_b, NT)

        def end_row(g, scores):
            here = slice(g * size, (g + 1) * size)
            shares, totals = [], 0.0
            for h in range(heads):
                score = jnp.where(same_row, scores[h * size : (h + 1) * size], -1e30)
                score = jnp.exp2(score - jnp.max(score, axis=1, keepdims=True))
                shares.append(score)
                totals = totals + jnp.sum(score, axis=1, keepdims=True) * head_mask[h]
            pooled = wide3(
                jnp.concatenate(shares, axis=1),
                jnp.concatenate([heads_of(value_h[here]), heads_of(value_m[here])], axis=1),
            )
            return pooled / totals

        mixed = pipelined(list(range(sub // rows)), 4, begin_row, end_row)
        mixed = jnp.concatenate(mixed, axis=0)
        row_state = x + fold(bdot(left4(mixed), out4[...], NN))
        v = bdot(left3(layer_norm(row_state)), up4[...], NN) + mlp_bias[...]
        hidden = v * (1.0 + jnp.tanh(v * (cube + (cube * 0.044715) * (v * v))))
        out[pl.ds(start * columns, sub * columns), :] = row_state + wide3(hidden, down3[...])

    def middle_row(s, carry):
        row_step(mid_arrived, s, s + 1, first_of(s), mid)
        return carry

    row_step(edge_arrived, 0, 0, 0, edge)
    if n_mid:
        lax.fori_loop(0, n_mid, middle_row, 0)
    for e in range(1, n_edge):
        row_step(edge_arrived, e, n_mid + e, row_count - (n_edge - e) * edge, edge)

    def drain(state, s, index, start, sub):
        pltpu.make_async_copy(
            state.at[s, pl.ds(0, n_col - 1)], state.at[s, pl.ds(0, n_col - 1)], cell_send.at[index]
        ).wait()

    def middle_drain(s, carry):
        drain(mid_state, s, s + 1, first_of(s), mid)
        return carry

    drain(edge_state, 0, 0, 0, edge)
    if n_mid:
        lax.fori_loop(0, n_mid, middle_drain, 0)
    for e in range(1, n_edge):
        drain(edge_state, e, n_mid + e, row_count - (n_edge - e) * edge, edge)


def body(
    cells,
    inducing,
    col_kv,
    col_query,
    col_out,
    back_query,
    back_kv,
    back_out,
    row_qkv,
    row_out,
    mlp_up,
    mlp_bias,
    mlp_down,
    scales,
):
    row_dev, col_dev, width = cells.shape
    heads = scales.shape[1]
    count = inducing.shape[0]
    n_col = lax.axis_size("col")
    n_row = lax.axis_size("row")
    row_count = row_dev // n_col
    columns = n_col * col_dev
    edge, n_edge, mid, n_mid = plan(row_count)
    chunks = n_edge + n_mid
    hidden = mlp_up.shape[1]
    vmem = pl.BlockSpec(memory_space=pltpu.VMEM)
    hbm = pl.BlockSpec(memory_space=pl.ANY)
    sizes = (n_col, n_row, row_dev, col_dev, width, heads, count)
    peers = max(1, n_row - 1)
    encoded = pl.pallas_call(
        functools.partial(kernel, sizes),
        out_shape=pltpu.VMEM((row_count * columns, width), f32),
        in_specs=[pl.BlockSpec(memory_space=pltpu.SMEM), hbm]
        + [vmem] * 7
        + [hbm] * 3
        + [vmem, hbm],
        out_specs=vmem,
        scratch_shapes=[
            pltpu.VMEM((row_dev * col_dev, width), f32),
            pltpu.VMEM((width, 3 * width), f32),
            pltpu.VMEM((width, width), f32),
            pltpu.VMEM((width, hidden), f32),
            pltpu.VMEM((hidden, width), f32),
            pltpu.VMEM((col_dev, n_col, row_count, width), f32),
            pltpu.VMEM((6 * width, 2 * heads * width), bf16),
            pltpu.VMEM((heads * count, width), f32),
            pltpu.VMEM((heads * count, width), f32),
            pltpu.VMEM((col_dev, heads * count, 6 * width), bf16),
            pltpu.VMEM((col_dev, heads * count, 2 * width), bf16),
            pltpu.VMEM((3, col_dev, count, width), f32),
            pltpu.VMEM((peers, 3, col_dev, count, width), f32),
            pltpu.VMEM((n_edge, n_col, col_dev, edge, width), f32),
            pltpu.VMEM((n_edge, n_col, col_dev, edge, width), f32),
            pltpu.VMEM((max(1, n_mid), n_col, col_dev, mid, width), f32),
            pltpu.VMEM((max(1, n_mid), n_col, col_dev, mid, width), f32),
            pltpu.VMEM((3 * width, hidden), bf16),
            pltpu.VMEM((6 * width, 2 * width), bf16),
            pltpu.VMEM((2 * width, 2 * width), bf16),
            pltpu.VMEM((2 * width, 2 * width), bf16),
            pltpu.VMEM((hidden, 2 * width), bf16),
            pltpu.SemaphoreType.DMA((5,)),
            pltpu.SemaphoreType.DMA((peers,)),
            pltpu.SemaphoreType.DMA((peers,)),
            pltpu.SemaphoreType.DMA((chunks,)),
            pltpu.SemaphoreType.DMA((chunks,)),
        ],
        compiler_params=pltpu.CompilerParams(
            collective_id=0, has_side_effects=True, vmem_limit_bytes=60 * 1024 * 1024
        ),
    )(
        scales,
        cells.reshape(row_dev * col_dev, width),
        inducing,
        col_kv,
        col_query,
        col_out,
        back_query,
        back_kv,
        back_out,
        row_qkv,
        row_out,
        mlp_up,
        mlp_bias.reshape(1, hidden),
        mlp_down,
    )
    return encoded.reshape(1, row_count, columns, width)


def solution(mesh):
    placed = (P("row", "col", None),) + (P(),) * 13
    return jax.shard_map(
        body, mesh=mesh, in_specs=placed, out_specs=P("row", "col", None, None), check_vma=False
    )
```

```python
import functools
import math

import jax
import jax.numpy as jnp
from jax import lax
from jax.experimental import pallas as pl
from jax.experimental.pallas import tpu as pltpu
from jax.sharding import PartitionSpec as P

epsilon = 1e-05
MESH = pl.DeviceIdType.MESH
bf16 = jnp.bfloat16
f32 = jnp.float32

NN = (((1,), (0,)), ((), ()))
NT = (((1,), (1,)), ((), ()))


def split2(x):
    hi = x.astype(bf16)
    return hi, (x - hi.astype(f32)).astype(bf16)


def split3(x):
    hi = x.astype(bf16)
    rest = x - hi.astype(f32)
    mid = rest.astype(bf16)
    return hi, mid, (rest - mid.astype(f32)).astype(bf16)


def bdot(a, b, dims):
    return lax.dot_general(a, b, dims, preferred_element_type=f32)


def left6(x):
    h, m, l = split3(x)
    return jnp.concatenate([h, m, h, m, h, l], axis=1)


def right6(x, axis):
    h, m, l = split3(x)
    return jnp.concatenate([h, h, m, m, l, h], axis=axis)


def lefts(x):
    h, m, l = split3(x)
    return jnp.concatenate([h, m], axis=1), jnp.concatenate([h, l], axis=1)


def rights(x, k):
    h, m, l = split3(x)
    both = jnp.concatenate([h, m], axis=1 - k)
    return jnp.concatenate([both, both], axis=k), jnp.concatenate([l, h], axis=k)


def fold(x):
    n = x.shape[1] // 2
    return x[:, :n] + x[:, n:]


def narrow6(left, right, dims):
    return fold(bdot(left[0], right[0], dims)) + bdot(left[1], right[1], dims)


def dot6(a, b):
    return narrow6(lefts(a), rights(b, 0), NN)


def dot6_nt(a, b):
    return narrow6(lefts(a), rights(b, 1), NT)


def left4(x):
    return jnp.concatenate(split2(x), axis=1)


def right4(x):
    both = jnp.concatenate(split2(x), axis=1)
    return jnp.concatenate([both, both], axis=0)


def left3(x):
    h, m = split2(x)
    return jnp.concatenate([h, m, h], axis=1)


def right3(x):
    h, m = split2(x)
    return jnp.concatenate([h, h, m], axis=0)


def dot3(a, b):
    return bdot(left3(a), right3(b), NN)


def wide3(a, right_both):
    n = right_both.shape[1] // 2
    h, m = split2(a)
    both = bdot(h, right_both, NN)
    return both[:, :n] + both[:, n:] + bdot(m, right_both[:, :n], NN)


def pipelined(units, ahead, begin, end):
    started, finished = [], []
    for k, unit in enumerate(units):
        started.append(begin(unit))
        if k >= ahead:
            finished.append(end(units[k - ahead], started[k - ahead]))
    for k in range(max(0, len(units) - ahead), len(units)):
        finished.append(end(units[k], started[k]))
    return finished


def layer_norm(values):
    centered = values - jnp.mean(values, axis=-1, keepdims=True)
    return centered * lax.rsqrt(jnp.mean(centered * centered, axis=-1, keepdims=True) + epsilon)


def plan(row_count):
    if row_count % 8:
        return row_count, 1, row_count, 0
    if row_count <= 16 or row_count % 16:
        return 8, row_count // 8, 8, 0
    return 8, 2, 16, (row_count - 16) // 16


def kernel(
    sizes,
    scales,
    cells_in,
    inducing,
    col_kv,
    col_query,
    col_out,
    back_query,
    back_kv,
    back_out,
    row_qkv_in,
    row_out_in,
    mlp_up_in,
    mlp_bias,
    mlp_down_in,
    out,
    cells,
    row_qkv,
    row_out,
    mlp_up,
    mlp_down,
    normed,
    fold6,
    base_left,
    base_right,
    back_left,
    back_right,
    mine,
    theirs,
    edge_state,
    edge_arrived,
    mid_state,
    mid_arrived,
    up4,
    qk6,
    value4,
    out4,
    down3,
    in_sem,
    stat_send,
    stat_recv,
    cell_send,
    cell_recv,
):
    n_col, n_row, row_dev, col_dev, width, heads, count = sizes
    head_size = width // heads
    row_count = row_dev // n_col
    columns = n_col * col_dev
    edge, n_edge, mid, n_mid = plan(row_count)
    me = lax.axis_index("col")
    group = lax.axis_index("row")
    root = math.log2(math.e) / math.sqrt(head_size)

    loads = [
        pltpu.make_async_copy(source, target, in_sem.at[k])
        for k, (source, target) in enumerate(
            (
                (cells_in, cells),
                (row_qkv_in, row_qkv),
                (row_out_in, row_out),
                (mlp_up_in, mlp_up),
                (mlp_down_in, mlp_down),
            )
        )
    ]
    loads[0].start()

    barrier = pltpu.get_barrier_semaphore()

    def greet(k, carry):
        pl.semaphore_signal(
            barrier, inc=1, device_id={"col": lax.rem(me + k, n_col)}, device_id_type=MESH
        )
        return carry

    lax.fori_loop(1, n_col, greet, 0)
    for k in range(1, n_row):
        pl.semaphore_signal(
            barrier, inc=1, device_id={"row": lax.rem(group + k, n_row)}, device_id_type=MESH
        )
    for load in loads[1:]:
        load.start()

    lane_head = lax.broadcasted_iota(jnp.int32, (1, width), 1) // head_size
    head_mask = [(lane_head == h).astype(f32) for h in range(heads)]

    def blocks(x, row):
        return jnp.concatenate(
            [x * (head_mask[h] * (scales[row, h] * root)) for h in range(heads)], axis=0
        )

    def plain_blocks(x):
        return jnp.concatenate([x * head_mask[h] for h in range(heads)], axis=0)

    query = dot6(inducing[...], col_query[...])
    score_left = left6(dot6_nt(blocks(query, 0), col_kv[:, :width]))
    value_weight = rights(col_kv[:, width:], 0)
    loads[0].wait()

    def begin_pool(c):
        column = layer_norm(cells[pl.ds(c, row_dev, stride=col_dev), :])
        normed[c] = column.reshape(n_col, row_count, width)
        return column, bdot(score_left, right6(column, 1), NT)

    def end_pool(c, begun):
        column, scores = begun
        peak = jnp.max(scores, axis=1, keepdims=True)
        weights = jnp.exp2(scores - peak)
        total = jnp.sum(weights, axis=1, keepdims=True)
        return wide3(weights, jnp.concatenate(split2(column), axis=1)), total, peak

    def gather_heads(x):
        return sum(x[h * count : (h + 1) * count] * head_mask[h] for h in range(heads))

    pooled = pipelined(list(range(col_dev)), 1, begin_pool, end_pool)
    for c in range(col_dev):
        values, total, peak = pooled[c]
        mine[0, c] = gather_heads(narrow6(lefts(values), value_weight, NN))
        mine[1, c] = gather_heads(total)
        mine[2, c] = gather_heads(peak)

    pl.semaphore_wait(barrier, n_col - 1 + n_row - 1)

    stat_copies = []
    for k in range(1, n_row):
        copy = pltpu.make_async_remote_copy(
            src_ref=mine,
            dst_ref=theirs.at[k - 1],
            send_sem=stat_send.at[k - 1],
            recv_sem=stat_recv.at[k - 1],
            device_id={"row": lax.rem(group + k, n_row)},
            device_id_type=MESH,
        )
        copy.start()
        stat_copies.append(copy)

    both = dot6(jnp.concatenate([col_out[...], inducing[...]], axis=0), back_kv[...])
    keys = dot6_nt(blocks(both[:, :width], 1), back_query[...])
    moves = dot6(plain_blocks(both[:, width:]), back_out[...])

    def part(x, h, k):
        start = h * (width + count) + k * width
        return x[start : start + (count if k else width)]

    for h in range(heads):
        base_left[h * count : (h + 1) * count] = part(keys, h, 1)
        base_right[h * count : (h + 1) * count] = part(moves, h, 1)
    fold6[...] = right6(
        jnp.concatenate(
            [part(keys, h, 0) for h in range(heads)] + [part(moves, h, 0) for h in range(heads)],
            axis=1,
        ),
        0,
    )

    for copy in stat_copies:
        copy.wait()

    joined = []
    for c in range(col_dev):
        top = mine[2, c]
        for k in range(n_row - 1):
            top = jnp.maximum(top, theirs[k, 2, c])
        factor = jnp.exp2(mine[2, c] - top)
        sums, total = mine[0, c] * factor, mine[1, c] * factor
        for k in range(n_row - 1):
            factor = jnp.exp2(theirs[k, 2, c] - top)
            sums = sums + theirs[k, 0, c] * factor
            total = total + theirs[k, 1, c] * factor
        joined.append(sums / total)
    products = bdot(left6(jnp.concatenate(joined, axis=0)), fold6[...], NN)
    for c in range(col_dev):
        product = products[c * count : (c + 1) * count]
        back_left[c] = right6(
            base_left[...]
            + jnp.concatenate(
                [product[:, h * width : (h + 1) * width] for h in range(heads)], axis=0
            ),
            1,
        )
        back_right[c] = jnp.concatenate(
            split2(
                base_right[...]
                + jnp.concatenate(
                    [product[:, (heads + h) * width : (heads + h + 1) * width] for h in range(heads)],
                    axis=0,
                )
            ),
            axis=1,
        )

    def cell_copy(state, arrived, s, index, k):
        peer = lax.rem(me + k, n_col)
        return pltpu.make_async_remote_copy(
            src_ref=state.at[s, peer],
            dst_ref=arrived.at[s, me],
            send_sem=cell_send.at[index],
            recv_sem=cell_recv.at[index],
            device_id={"col": peer},
            device_id_type=MESH,
        )

    def back_step(state, arrived, s, index, start, sub):
        def begin_back(c):
            block = normed[c, :, pl.ds(start, sub), :].reshape(n_col * sub, width)
            return block, bdot(left6(block), back_left[c], NT)

        def end_back(c, begun):
            block, scores = begun
            shares = []
            for h in range(heads):
                part = scores[:, h * count : (h + 1) * count]
                part = jnp.exp2(part - jnp.max(part, axis=1, keepdims=True))
                shares.append(part * (1.0 / jnp.sum(part, axis=1, keepdims=True)))
            moved = block + wide3(jnp.concatenate(shares, axis=1), back_right[c])
            state[s, :, c] = moved.reshape(n_col, sub, width)

        pipelined(list(range(col_dev)), 1, begin_back, end_back)

        def send(k, inner):
            cell_copy(state, arrived, s, index, k).start()
            return inner

        lax.fori_loop(1, n_col, send, 0)
        arrived[s, me] = state[s, me]

    def first_of(s):
        return pl.multiple_of(edge + s * mid, 8)

    def middle_back(s, carry):
        back_step(mid_state, mid_arrived, s, s + 1, first_of(s), mid)
        return carry

    back_step(edge_state, edge_arrived, 0, 0, 0, edge)
    if n_mid:
        lax.fori_loop(0, n_mid, middle_back, 0)
    for e in range(1, n_edge):
        start = row_count - (n_edge - e) * edge
        back_step(edge_state, edge_arrived, e, n_mid + e, start, edge)

    for load in loads[1:]:
        load.wait()
    qkv = row_qkv[...]
    row_scale = sum(head_mask[h] * (scales[2, h] * root) for h in range(heads))
    qk6[...] = right6(
        jnp.concatenate([qkv[:, :width] * row_scale, qkv[:, width : 2 * width]], axis=1), 0
    )
    value4[...] = right4(qkv[:, 2 * width :])
    out4[...] = right4(row_out[...])
    up_h, up_m = split2(mlp_up[...])
    up4[...] = jnp.concatenate([up_h, up_h, up_m], axis=0)
    down3[...] = jnp.concatenate(split2(0.5 * mlp_down[...]), axis=1)

    rows = max(1, 128 // columns)
    size = rows * columns
    place = lax.broadcasted_iota(jnp.int32, (size, size), 0) // columns
    other = lax.broadcasted_iota(jnp.int32, (size, size), 1) // columns
    same_row = place == other
    cube = math.sqrt(2.0 / math.pi)
    bf_mask = [m.astype(bf16) for m in head_mask]

    def heads_of(x):
        return jnp.concatenate([x * bf_mask[h] for h in range(heads)], axis=0)

    def row_step(arrived, s, index, start, sub):
        pltpu.make_async_copy(
            arrived.at[s, pl.ds(0, n_col - 1)],
            arrived.at[s, pl.ds(0, n_col - 1)],
            cell_recv.at[index],
        ).wait()
        flat = arrived.at[s].reshape(columns * sub, width)
        x = jnp.concatenate(
            [flat[pl.ds(r, columns, stride=sub), :] for r in range(sub)], axis=0
        )
        h, m, l = split3(layer_norm(x))
        both = jnp.concatenate([h, m], axis=1)
        query_keys = bdot(jnp.concatenate([both, both, h, l], axis=1), qk6[...], NN)
        query_h, query_m, query_l = split3(query_keys[:, :width])
        key_h, key_m, key_l = split3(query_keys[:, width:])
        value_h, value_m = split2(fold(bdot(both, value4[...], NN)))

        def begin_row(g):
            here = slice(g * size, (g + 1) * size)
            left_h = heads_of(query_h[here])
            left_a = jnp.concatenate([left_h, heads_of(query_m[here])], axis=1)
            left_b = jnp.concatenate([left_h, heads_of(query_l[here])], axis=1)
            right_a = jnp.concatenate([key_h[here], key_m[here]], axis=0)
            right_a = jnp.concatenate([right_a, right_a], axis=1)
            right_b = jnp.concatenate([key_l[here], key_h[here]], axis=1)
            return fold(bdot(left_a, right_a, NT)) + bdot(left_b, right_b, NT)

        def end_row(g, scores):
            here = slice(g * size, (g + 1) * size)
            shares, totals = [], 0.0
            for h in range(heads):
                score = jnp.where(same_row, scores[h * size : (h + 1) * size], -1e30)
                score = jnp.exp2(score - jnp.max(score, axis=1, keepdims=True))
                shares.append(score)
                totals = totals + jnp.sum(score, axis=1, keepdims=True) * head_mask[h]
            pooled = wide3(
                jnp.concatenate(shares, axis=1),
                jnp.concatenate([heads_of(value_h[here]), heads_of(value_m[here])], axis=1),
            )
            return pooled / totals

        mixed = pipelined(list(range(sub // rows)), 4, begin_row, end_row)
        mixed = jnp.concatenate(mixed, axis=0)
        row_state = x + fold(bdot(left4(mixed), out4[...], NN))
        v = bdot(left3(layer_norm(row_state)), up4[...], NN) + mlp_bias[...]
        hidden = v * (1.0 + jnp.tanh(v * (cube + (cube * 0.044715) * (v * v))))
        out[pl.ds(start * columns, sub * columns), :] = row_state + wide3(hidden, down3[...])

    def middle_row(s, carry):
        row_step(mid_arrived, s, s + 1, first_of(s), mid)
        return carry

    row_step(edge_arrived, 0, 0, 0, edge)
    if n_mid:
        lax.fori_loop(0, n_mid, middle_row, 0)
    for e in range(1, n_edge):
        row_step(edge_arrived, e, n_mid + e, row_count - (n_edge - e) * edge, edge)

    def drain(state, s, index, start, sub):
        pltpu.make_async_copy(
            state.at[s, pl.ds(0, n_col - 1)], state.at[s, pl.ds(0, n_col - 1)], cell_send.at[index]
        ).wait()

    def middle_drain(s, carry):
        drain(mid_state, s, s + 1, first_of(s), mid)
        return carry

    drain(edge_state, 0, 0, 0, edge)
    if n_mid:
        lax.fori_loop(0, n_mid, middle_drain, 0)
    for e in range(1, n_edge):
        drain(edge_state, e, n_mid + e, row_count - (n_edge - e) * edge, edge)


def body(
    cells,
    inducing,
    col_kv,
    col_query,
    col_out,
    back_query,
    back_kv,
    back_out,
    row_qkv,
    row_out,
    mlp_up,
    mlp_bias,
    mlp_down,
    scales,
):
    row_dev, col_dev, width = cells.shape
    heads = scales.shape[1]
    count = inducing.shape[0]
    n_col = lax.axis_size("col")
    n_row = lax.axis_size("row")
    row_count = row_dev // n_col
    columns = n_col * col_dev
    edge, n_edge, mid, n_mid = plan(row_count)
    chunks = n_edge + n_mid
    hidden = mlp_up.shape[1]
    vmem = pl.BlockSpec(memory_space=pltpu.VMEM)
    hbm = pl.BlockSpec(memory_space=pl.ANY)
    sizes = (n_col, n_row, row_dev, col_dev, width, heads, count)
    peers = max(1, n_row - 1)
    encoded = pl.pallas_call(
        functools.partial(kernel, sizes),
        out_shape=pltpu.VMEM((row_count * columns, width), f32),
        in_specs=[pl.BlockSpec(memory_space=pltpu.SMEM), hbm]
        + [vmem] * 7
        + [hbm] * 3
        + [vmem, hbm],
        out_specs=vmem,
        scratch_shapes=[
            pltpu.VMEM((row_dev * col_dev, width), f32),
            pltpu.VMEM((width, 3 * width), f32),
            pltpu.VMEM((width, width), f32),
            pltpu.VMEM((width, hidden), f32),
            pltpu.VMEM((hidden, width), f32),
            pltpu.VMEM((col_dev, n_col, row_count, width), f32),
            pltpu.VMEM((6 * width, 2 * heads * width), bf16),
            pltpu.VMEM((heads * count, width), f32),
            pltpu.VMEM((heads * count, width), f32),
            pltpu.VMEM((col_dev, heads * count, 6 * width), bf16),
            pltpu.VMEM((col_dev, heads * count, 2 * width), bf16),
            pltpu.VMEM((3, col_dev, count, width), f32),
            pltpu.VMEM((peers, 3, col_dev, count, width), f32),
            pltpu.VMEM((n_edge, n_col, col_dev, edge, width), f32),
            pltpu.VMEM((n_edge, n_col, col_dev, edge, width), f32),
            pltpu.VMEM((max(1, n_mid), n_col, col_dev, mid, width), f32),
            pltpu.VMEM((max(1, n_mid), n_col, col_dev, mid, width), f32),
            pltpu.VMEM((3 * width, hidden), bf16),
            pltpu.VMEM((6 * width, 2 * width), bf16),
            pltpu.VMEM((2 * width, 2 * width), bf16),
            pltpu.VMEM((2 * width, 2 * width), bf16),
            pltpu.VMEM((hidden, 2 * width), bf16),
            pltpu.SemaphoreType.DMA((5,)),
            pltpu.SemaphoreType.DMA((peers,)),
            pltpu.SemaphoreType.DMA((peers,)),
            pltpu.SemaphoreType.DMA((chunks,)),
            pltpu.SemaphoreType.DMA((chunks,)),
        ],
        compiler_params=pltpu.CompilerParams(
            collective_id=0, has_side_effects=True, vmem_limit_bytes=60 * 1024 * 1024
        ),
    )(
        scales,
        cells.reshape(row_dev * col_dev, width),
        inducing,
        col_kv,
        col_query,
        col_out,
        back_query,
        back_kv,
        back_out,
        row_qkv,
        row_out,
        mlp_up,
        mlp_bias.reshape(1, hidden),
        mlp_down,
    )
    return encoded.reshape(1, row_count, columns, width)


def solution(mesh):
    placed = (P("row", "col", None),) + (P(),) * 13
    return jax.shard_map(
        body, mesh=mesh, in_specs=placed, out_specs=P("row", "col", None, None), check_vma=False
    )
```

```python
import functools
import math

import jax
import jax.numpy as jnp
from jax import lax
from jax.experimental import pallas as pl
from jax.experimental.pallas import tpu as pltpu
from jax.sharding import PartitionSpec as P

epsilon = 1e-05
MESH = pl.DeviceIdType.MESH
bf16 = jnp.bfloat16
f32 = jnp.float32

NN = (((1,), (0,)), ((), ()))
NT = (((1,), (1,)), ((), ()))


def split2(x):
    hi = x.astype(bf16)
    return hi, (x - hi.astype(f32)).astype(bf16)


def split3(x):
    hi = x.astype(bf16)
    rest = x - hi.astype(f32)
    mid = rest.astype(bf16)
    return hi, mid, (rest - mid.astype(f32)).astype(bf16)


def bdot(a, b, dims):
    return lax.dot_general(a, b, dims, preferred_element_type=f32)


def left6(x):
    h, m, l = split3(x)
    return jnp.concatenate([h, m, h, m, h, l], axis=1)


def right6(x, axis):
    h, m, l = split3(x)
    return jnp.concatenate([h, h, m, m, l, h], axis=axis)


def lefts(x):
    h, m, l = split3(x)
    return jnp.concatenate([h, m], axis=1), jnp.concatenate([h, l], axis=1)


def rights(x, k):
    h, m, l = split3(x)
    both = jnp.concatenate([h, m], axis=1 - k)
    return jnp.concatenate([both, both], axis=k), jnp.concatenate([l, h], axis=k)


def fold(x):
    n = x.shape[1] // 2
    return x[:, :n] + x[:, n:]


def narrow6(left, right, dims):
    return fold(bdot(left[0], right[0], dims)) + bdot(left[1], right[1], dims)


def dot6(a, b):
    return narrow6(lefts(a), rights(b, 0), NN)


def dot6_nt(a, b):
    return narrow6(lefts(a), rights(b, 1), NT)


def left4(x):
    return jnp.concatenate(split2(x), axis=1)


def right4(x):
    both = jnp.concatenate(split2(x), axis=1)
    return jnp.concatenate([both, both], axis=0)


def left3(x):
    h, m = split2(x)
    return jnp.concatenate([h, m, h], axis=1)


def right3(x):
    h, m = split2(x)
    return jnp.concatenate([h, h, m], axis=0)


def dot3(a, b):
    return bdot(left3(a), right3(b), NN)


def wide3(a, right_both):
    n = right_both.shape[1] // 2
    h, m = split2(a)
    both = bdot(h, right_both, NN)
    return both[:, :n] + both[:, n:] + bdot(m, right_both[:, :n], NN)


def pipelined(units, ahead, begin, end):
    started, finished = [], []
    for k, unit in enumerate(units):
        started.append(begin(unit))
        if k >= ahead:
            finished.append(end(units[k - ahead], started[k - ahead]))
    for k in range(max(0, len(units) - ahead), len(units)):
        finished.append(end(units[k], started[k]))
    return finished


def layer_norm(values):
    centered = values - jnp.mean(values, axis=-1, keepdims=True)
    return centered * lax.rsqrt(jnp.mean(centered * centered, axis=-1, keepdims=True) + epsilon)


def plan(row_count):
    if row_count % 8:
        return row_count, 1, row_count, 0
    if row_count <= 16 or row_count % 16:
        return 8, row_count // 8, 8, 0
    if (row_count - 16) % 24 == 0:
        return 8, 2, 24, (row_count - 16) // 24
    return 8, 2, 16, (row_count - 16) // 16


def kernel(
    sizes,
    scales,
    cells_in,
    inducing,
    col_kv,
    col_query,
    col_out,
    back_query,
    back_kv,
    back_out,
    row_qkv_in,
    row_out_in,
    mlp_up_in,
    mlp_bias,
    mlp_down_in,
    out,
    cells,
    row_qkv,
    row_out,
    mlp_up,
    mlp_down,
    normed,
    fold6,
    base_left,
    base_right,
    back_left,
    back_right,
    mine,
    theirs,
    edge_state,
    edge_arrived,
    mid_state,
    mid_arrived,
    up4,
    qk6,
    value4,
    out4,
    down3,
    in_sem,
    stat_send,
    stat_recv,
    cell_send,
    cell_recv,
):
    n_col, n_row, row_dev, col_dev, width, heads, count = sizes
    head_size = width // heads
    row_count = row_dev // n_col
    columns = n_col * col_dev
    edge, n_edge, mid, n_mid = plan(row_count)
    me = lax.axis_index("col")
    group = lax.axis_index("row")
    root = math.log2(math.e) / math.sqrt(head_size)

    loads = [
        pltpu.make_async_copy(source, target, in_sem.at[k])
        for k, (source, target) in enumerate(
            (
                (cells_in, cells),
                (row_qkv_in, row_qkv),
                (row_out_in, row_out),
                (mlp_up_in, mlp_up),
                (mlp_down_in, mlp_down),
            )
        )
    ]
    loads[0].start()

    barrier = pltpu.get_barrier_semaphore()

    def greet(k, carry):
        pl.semaphore_signal(
            barrier, inc=1, device_id={"col": lax.rem(me + k, n_col)}, device_id_type=MESH
        )
        return carry

    lax.fori_loop(1, n_col, greet, 0)
    for k in range(1, n_row):
        pl.semaphore_signal(
            barrier, inc=1, device_id={"row": lax.rem(group + k, n_row)}, device_id_type=MESH
        )
    for load in loads[1:]:
        load.start()

    lane_head = lax.broadcasted_iota(jnp.int32, (1, width), 1) // head_size
    head_mask = [(lane_head == h).astype(f32) for h in range(heads)]

    def blocks(x, row):
        return jnp.concatenate(
            [x * (head_mask[h] * (scales[row, h] * root)) for h in range(heads)], axis=0
        )

    def plain_blocks(x):
        return jnp.concatenate([x * head_mask[h] for h in range(heads)], axis=0)

    query = dot6(inducing[...], col_query[...])
    score_left = left6(dot6_nt(blocks(query, 0), col_kv[:, :width]))
    value_weight = rights(col_kv[:, width:], 0)
    loads[0].wait()

    def begin_pool(c):
        column = layer_norm(cells[pl.ds(c, row_dev, stride=col_dev), :])
        normed[c] = column.reshape(n_col, row_count, width)
        return column, bdot(score_left, right6(column, 1), NT)

    def end_pool(c, begun):
        column, scores = begun
        peak = jnp.max(scores, axis=1, keepdims=True)
        weights = jnp.exp2(scores - peak)
        total = jnp.sum(weights, axis=1, keepdims=True)
        return wide3(weights, jnp.concatenate(split2(column), axis=1)), total, peak

    def gather_heads(x):
        return sum(x[h * count : (h + 1) * count] * head_mask[h] for h in range(heads))

    pooled = pipelined(list(range(col_dev)), 1, begin_pool, end_pool)
    for c in range(col_dev):
        values, total, peak = pooled[c]
        mine[0, c] = gather_heads(narrow6(lefts(values), value_weight, NN))
        mine[1, c] = gather_heads(total)
        mine[2, c] = gather_heads(peak)

    pl.semaphore_wait(barrier, n_col - 1 + n_row - 1)

    stat_copies = []
    for k in range(1, n_row):
        copy = pltpu.make_async_remote_copy(
            src_ref=mine,
            dst_ref=theirs.at[k - 1],
            send_sem=stat_send.at[k - 1],
            recv_sem=stat_recv.at[k - 1],
            device_id={"row": lax.rem(group + k, n_row)},
            device_id_type=MESH,
        )
        copy.start()
        stat_copies.append(copy)

    both = dot6(jnp.concatenate([col_out[...], inducing[...]], axis=0), back_kv[...])
    keys = dot6_nt(blocks(both[:, :width], 1), back_query[...])
    moves = dot6(plain_blocks(both[:, width:]), back_out[...])

    def part(x, h, k):
        start = h * (width + count) + k * width
        return x[start : start + (count if k else width)]

    for h in range(heads):
        base_left[h * count : (h + 1) * count] = part(keys, h, 1)
        base_right[h * count : (h + 1) * count] = part(moves, h, 1)
    fold6[...] = right6(
        jnp.concatenate(
            [part(keys, h, 0) for h in range(heads)] + [part(moves, h, 0) for h in range(heads)],
            axis=1,
        ),
        0,
    )

    for copy in stat_copies:
        copy.wait()

    joined = []
    for c in range(col_dev):
        top = mine[2, c]
        for k in range(n_row - 1):
            top = jnp.maximum(top, theirs[k, 2, c])
        factor = jnp.exp2(mine[2, c] - top)
        sums, total = mine[0, c] * factor, mine[1, c] * factor
        for k in range(n_row - 1):
            factor = jnp.exp2(theirs[k, 2, c] - top)
            sums = sums + theirs[k, 0, c] * factor
            total = total + theirs[k, 1, c] * factor
        joined.append(sums / total)
    products = bdot(left6(jnp.concatenate(joined, axis=0)), fold6[...], NN)
    for c in range(col_dev):
        product = products[c * count : (c + 1) * count]
        back_left[c] = right6(
            base_left[...]
            + jnp.concatenate(
                [product[:, h * width : (h + 1) * width] for h in range(heads)], axis=0
            ),
            1,
        )
        back_right[c] = jnp.concatenate(
            split2(
                base_right[...]
                + jnp.concatenate(
                    [product[:, (heads + h) * width : (heads + h + 1) * width] for h in range(heads)],
                    axis=0,
                )
            ),
            axis=1,
        )

    def cell_copy(state, arrived, s, index, k):
        peer = lax.rem(me + k, n_col)
        return pltpu.make_async_remote_copy(
            src_ref=state.at[s, peer],
            dst_ref=arrived.at[s, me],
            send_sem=cell_send.at[index],
            recv_sem=cell_recv.at[index],
            device_id={"col": peer},
            device_id_type=MESH,
        )

    def back_step(state, arrived, s, index, start, sub):
        def begin_back(c):
            block = normed[c, :, pl.ds(start, sub), :].reshape(n_col * sub, width)
            return block, bdot(left6(block), back_left[c], NT)

        def end_back(c, begun):
            block, scores = begun
            shares = []
            for h in range(heads):
                part = scores[:, h * count : (h + 1) * count]
                part = jnp.exp2(part - jnp.max(part, axis=1, keepdims=True))
                shares.append(part * (1.0 / jnp.sum(part, axis=1, keepdims=True)))
            moved = block + wide3(jnp.concatenate(shares, axis=1), back_right[c])
            state[s, :, c] = moved.reshape(n_col, sub, width)

        pipelined(list(range(col_dev)), 1, begin_back, end_back)

        def send(k, inner):
            cell_copy(state, arrived, s, index, k).start()
            return inner

        lax.fori_loop(1, n_col, send, 0)
        arrived[s, me] = state[s, me]

    def first_of(s):
        return pl.multiple_of(edge + s * mid, 8)

    def middle_back(s, carry):
        back_step(mid_state, mid_arrived, s, s + 1, first_of(s), mid)
        return carry

    back_step(edge_state, edge_arrived, 0, 0, 0, edge)
    if n_mid:
        lax.fori_loop(0, n_mid, middle_back, 0)
    for e in range(1, n_edge):
        start = row_count - (n_edge - e) * edge
        back_step(edge_state, edge_arrived, e, n_mid + e, start, edge)

    for load in loads[1:]:
        load.wait()
    qkv = row_qkv[...]
    row_scale = sum(head_mask[h] * (scales[2, h] * root) for h in range(heads))
    qk6[...] = right6(
        jnp.concatenate([qkv[:, :width] * row_scale, qkv[:, width : 2 * width]], axis=1), 0
    )
    value4[...] = right4(qkv[:, 2 * width :])
    out4[...] = right4(row_out[...])
    up_h, up_m = split2(mlp_up[...])
    up4[...] = jnp.concatenate([up_h, up_h, up_m], axis=0)
    down3[...] = jnp.concatenate(split2(0.5 * mlp_down[...]), axis=1)

    rows = max(1, 128 // columns)
    size = rows * columns
    place = lax.broadcasted_iota(jnp.int32, (size, size), 0) // columns
    other = lax.broadcasted_iota(jnp.int32, (size, size), 1) // columns
    same_row = place == other
    cube = math.sqrt(2.0 / math.pi)
    bf_mask = [m.astype(bf16) for m in head_mask]

    def heads_of(x):
        return jnp.concatenate([x * bf_mask[h] for h in range(heads)], axis=0)

    def row_step(arrived, s, index, start, sub):
        pltpu.make_async_copy(
            arrived.at[s, pl.ds(0, n_col - 1)],
            arrived.at[s, pl.ds(0, n_col - 1)],
            cell_recv.at[index],
        ).wait()
        flat = arrived.at[s].reshape(columns * sub, width)
        x = jnp.concatenate(
            [flat[pl.ds(r, columns, stride=sub), :] for r in range(sub)], axis=0
        )
        h, m, l = split3(layer_norm(x))
        both = jnp.concatenate([h, m], axis=1)
        query_keys = bdot(jnp.concatenate([both, both, h, l], axis=1), qk6[...], NN)
        query_h, query_m, query_l = split3(query_keys[:, :width])
        key_h, key_m, key_l = split3(query_keys[:, width:])
        value_h, value_m = split2(fold(bdot(both, value4[...], NN)))

        def begin_row(g):
            here = slice(g * size, (g + 1) * size)
            left_h = heads_of(query_h[here])
            left_a = jnp.concatenate([left_h, heads_of(query_m[here])], axis=1)
            left_b = jnp.concatenate([left_h, heads_of(query_l[here])], axis=1)
            right_a = jnp.concatenate([key_h[here], key_m[here]], axis=0)
            right_a = jnp.concatenate([right_a, right_a], axis=1)
            right_b = jnp.concatenate([key_l[here], key_h[here]], axis=1)
            return fold(bdot(left_a, right_a, NT)) + bdot(left_b, right_b, NT)

        def end_row(g, scores):
            here = slice(g * size, (g + 1) * size)
            shares, totals = [], 0.0
            for h in range(heads):
                score = jnp.where(same_row, scores[h * size : (h + 1) * size], -1e30)
                score = jnp.exp2(score - jnp.max(score, axis=1, keepdims=True))
                shares.append(score)
                totals = totals + jnp.sum(score, axis=1, keepdims=True) * head_mask[h]
            pooled = wide3(
                jnp.concatenate(shares, axis=1),
                jnp.concatenate([heads_of(value_h[here]), heads_of(value_m[here])], axis=1),
            )
            return pooled / totals

        mixed = pipelined(list(range(sub // rows)), 4, begin_row, end_row)
        mixed = jnp.concatenate(mixed, axis=0)
        row_state = x + fold(bdot(left4(mixed), out4[...], NN))
        v = bdot(left3(layer_norm(row_state)), up4[...], NN) + mlp_bias[...]
        hidden = v * (1.0 + jnp.tanh(v * (cube + (cube * 0.044715) * (v * v))))
        out[pl.ds(start * columns, sub * columns), :] = row_state + wide3(hidden, down3[...])

    def middle_row(s, carry):
        row_step(mid_arrived, s, s + 1, first_of(s), mid)
        return carry

    row_step(edge_arrived, 0, 0, 0, edge)
    if n_mid:
        lax.fori_loop(0, n_mid, middle_row, 0)
    for e in range(1, n_edge):
        row_step(edge_arrived, e, n_mid + e, row_count - (n_edge - e) * edge, edge)

    def drain(state, s, index, start, sub):
        pltpu.make_async_copy(
            state.at[s, pl.ds(0, n_col - 1)], state.at[s, pl.ds(0, n_col - 1)], cell_send.at[index]
        ).wait()

    def middle_drain(s, carry):
        drain(mid_state, s, s + 1, first_of(s), mid)
        return carry

    drain(edge_state, 0, 0, 0, edge)
    if n_mid:
        lax.fori_loop(0, n_mid, middle_drain, 0)
    for e in range(1, n_edge):
        drain(edge_state, e, n_mid + e, row_count - (n_edge - e) * edge, edge)


def body(
    cells,
    inducing,
    col_kv,
    col_query,
    col_out,
    back_query,
    back_kv,
    back_out,
    row_qkv,
    row_out,
    mlp_up,
    mlp_bias,
    mlp_down,
    scales,
):
    row_dev, col_dev, width = cells.shape
    heads = scales.shape[1]
    count = inducing.shape[0]
    n_col = lax.axis_size("col")
    n_row = lax.axis_size("row")
    row_count = row_dev // n_col
    columns = n_col * col_dev
    edge, n_edge, mid, n_mid = plan(row_count)
    chunks = n_edge + n_mid
    hidden = mlp_up.shape[1]
    vmem = pl.BlockSpec(memory_space=pltpu.VMEM)
    hbm = pl.BlockSpec(memory_space=pl.ANY)
    sizes = (n_col, n_row, row_dev, col_dev, width, heads, count)
    peers = max(1, n_row - 1)
    encoded = pl.pallas_call(
        functools.partial(kernel, sizes),
        out_shape=pltpu.VMEM((row_count * columns, width), f32),
        in_specs=[pl.BlockSpec(memory_space=pltpu.SMEM), hbm]
        + [vmem] * 7
        + [hbm] * 3
        + [vmem, hbm],
        out_specs=vmem,
        scratch_shapes=[
            pltpu.VMEM((row_dev * col_dev, width), f32),
            pltpu.VMEM((width, 3 * width), f32),
            pltpu.VMEM((width, width), f32),
            pltpu.VMEM((width, hidden), f32),
            pltpu.VMEM((hidden, width), f32),
            pltpu.VMEM((col_dev, n_col, row_count, width), f32),
            pltpu.VMEM((6 * width, 2 * heads * width), bf16),
            pltpu.VMEM((heads * count, width), f32),
            pltpu.VMEM((heads * count, width), f32),
            pltpu.VMEM((col_dev, heads * count, 6 * width), bf16),
            pltpu.VMEM((col_dev, heads * count, 2 * width), bf16),
            pltpu.VMEM((3, col_dev, count, width), f32),
            pltpu.VMEM((peers, 3, col_dev, count, width), f32),
            pltpu.VMEM((n_edge, n_col, col_dev, edge, width), f32),
            pltpu.VMEM((n_edge, n_col, col_dev, edge, width), f32),
            pltpu.VMEM((max(1, n_mid), n_col, col_dev, mid, width), f32),
            pltpu.VMEM((max(1, n_mid), n_col, col_dev, mid, width), f32),
            pltpu.VMEM((3 * width, hidden), bf16),
            pltpu.VMEM((6 * width, 2 * width), bf16),
            pltpu.VMEM((2 * width, 2 * width), bf16),
            pltpu.VMEM((2 * width, 2 * width), bf16),
            pltpu.VMEM((hidden, 2 * width), bf16),
            pltpu.SemaphoreType.DMA((5,)),
            pltpu.SemaphoreType.DMA((peers,)),
            pltpu.SemaphoreType.DMA((peers,)),
            pltpu.SemaphoreType.DMA((chunks,)),
            pltpu.SemaphoreType.DMA((chunks,)),
        ],
        compiler_params=pltpu.CompilerParams(
            collective_id=0, has_side_effects=True, vmem_limit_bytes=60 * 1024 * 1024
        ),
    )(
        scales,
        cells.reshape(row_dev * col_dev, width),
        inducing,
        col_kv,
        col_query,
        col_out,
        back_query,
        back_kv,
        back_out,
        row_qkv,
        row_out,
        mlp_up,
        mlp_bias.reshape(1, hidden),
        mlp_down,
    )
    return encoded.reshape(1, row_count, columns, width)


def solution(mesh):
    placed = (P("row", "col", None),) + (P(),) * 13
    return jax.shard_map(
        body, mesh=mesh, in_specs=placed, out_specs=P("row", "col", None, None), check_vma=False
    )
```
